768 devices in a mesh: fsdp: 24 (over z, x_lo), expert: 32 (over x_hi, y, core).
Axes of the slice: x: 4 (x_hi: 2, x_lo: 2; x = x_hi * 2 + x_lo), y: 8, z: 12, core: 2. Of those that a mesh axis runs over, the one named last changes fastest.
Arguments:
- tokens: bfloat16 [2048, 6144], P('expert', 'fsdp'), may hold values from -6 to 6
- expert_ids: int32 [2048, 2], P('expert'), may hold values from 0 to 7, all different within a row; in each aligned block of 64 rows (0 to 63, 64 to 127, ...) at most 24 rows name the same one
- gate_values: float32 [2048, 2], P('expert'), may hold values from 0.1 to 1
- w_gate: bfloat16 [6144, 65536], P('fsdp', 'expert'), may hold values from -0.078125 to 0.078125
- w_up: bfloat16 [6144, 65536], P('fsdp', 'expert'), may hold values from -0.078125 to 0.078125
- w_down: bfloat16 [65536, 6144], P('expert', 'fsdp'), may hold values from -0.0625 to 0.0625
- scale_gate: float32 [48, 512], P('fsdp', 'expert'), may hold values from 0.5 to 2
- scale_up: float32 [48, 512], P('fsdp', 'expert'), may hold values from 0.5 to 2
- scale_down: float32 [512, 48], P('expert', 'fsdp'), may hold values from 0.5 to 2
Outputs:
- mixed: bfloat16 [2048, 6144], P('expert', 'fsdp')
The draws below stay inside these ranges and needn't reach their ends.
Inputs may be any that keep to these rules, and one draw needn't show every extreme that they name: `expert_ids`: within the 64 rows of each index of expert (aligned blocks of rows), no expert id occurs in more than 24 rows, and some id occurs in exactly 24 rows of some block; the two ids of a row differ; every id occurs somewhere.
All inputs are finite; a program needn't handle non-finite values.
Results may differ from the reference program's by a relative error of at most 0.03.
Values may be sent and summed in bfloat16 or wider, within the bound.
A program may use at most 32 MiB of HBM per device.

```python
import math
import jax
import jax.numpy as jnp
import numpy as np
from jax import lax

D = 6144
EXPERTS = 8
HIDDEN_SIZE = 8192
BLOCK = 128
TOK = 64
CAP = 24
TOKENS = 2048
N_FSDP = 24
N_EXPERT = 32


def shard_levels(rng, extent, split, low, largest):
    def one(dim, parts):
        steps = jax.random.uniform(jax.random.fold_in(jax.random.fold_in(rng, 6), dim), (parts,), jnp.float32, low / len(split), largest / len(split))
        return jnp.repeat(jnp.exp(steps), extent[dim] // parts).reshape((-1,) + (1,) * (len(extent) - dim - 1))

    gain = one(*split[0])
    for cut in split[1:]:
        gain = gain * one(*cut)
    return gain


def routed_block(stream_key, own, number, rows, count, top, bound, lean):
    order = jax.random.permutation(stream_key, count)
    crowded, ordinary = load_shares(count, rows * top, bound, lean, True), load_shares(count, rows * top, bound, lean, False)
    places = jnp.arange(count)

    def named(sizes, turn):
        used = int((sizes > 0).sum())
        fixed = max(1, used // 4)
        shifted = fixed + (places - fixed + turn * (used - fixed)) % max(1, count - fixed)
        return jnp.zeros((count,), jnp.int32).at[order[jnp.where(places < fixed, places, shifted)]].set(jnp.asarray(sizes, jnp.int32))

    sizes = jnp.where(number % 4 == 0, named(crowded, number // 4), named(ordinary, number - number // 4 - 1))
    mixed = jax.random.permutation(jax.random.fold_in(own, 3), count)
    source_of, receiver = mixed[0:count // 2 * 2:2], mixed[1:count // 2 * 2:2]
    margin = jnp.minimum(sizes[source_of] - 1, bound - sizes[receiver]) // 2
    margin = jnp.where((source_of == order[0]) | (receiver == order[0]) | (sizes[receiver] == 0), 0, jnp.maximum(margin, 0))
    shifted = jax.random.randint(jax.random.fold_in(own, 4), (count // 2,), 0, 1 << 20) % (margin + 1)
    sizes = sizes.at[source_of].add(-shifted).at[receiver].add(shifted)
    members = jnp.searchsorted(jnp.cumsum(sizes), jnp.arange(rows * top), side="right").astype(jnp.int32)
    table = members.reshape(top, rows).T
    table = table[jax.random.permutation(jax.random.fold_in(own, 1), rows)]
    turn = jax.random.randint(jax.random.fold_in(own, 2), (rows, 1), 0, top)
    return jnp.take_along_axis(table, (jnp.arange(top)[None, :] + turn) % top, axis=1)


def load_shares(number_of, total, bound, lean, full):
    weights = [(1 << 20) // math.isqrt(standing ** lean) + 1 for standing in range(1, number_of + 1)]
    largest = bound if full else min(bound, max(-(-total // number_of), total * weights[0] // sum(weights)))
    least = 1 if total - largest >= number_of - 1 else 0
    holding, rest = [largest] + [least] * (number_of - 1), total - largest - least * (number_of - 1)
    while rest > 0:
        free = [i for i in range(1, number_of) if holding[i] < largest] or [i for i in range(1, number_of) if holding[i] < bound]
        pool, left = sum([weights[i] for i in free]), rest
        for i in free:
            extra = min(bound - holding[i], max(1, left * weights[i] // pool), rest)
            holding[i] = holding[i] + extra
            rest = rest - extra
    return np.array(holding)


def bell_draw(key, dims, deviation, most, cuts=(), kind=jnp.bfloat16):
    factor_of = shard_levels(key, dims, cuts, -0.22, 0.18) if cuts else 1.0
    values = jax.random.normal(key, dims, jnp.float32) * deviation * factor_of
    return jnp.minimum(jnp.maximum(values, -most), most).astype(kind)


def setup_inputs(seed: int = 0) -> dict:
    arg_keys = jax.random.split(jax.random.key(seed), 10)
    tokens = bell_draw(arg_keys[0], (TOKENS, D), 1.0, 6.0, ((0, 32), (1, 24)))
    expert_ids_keys = jax.random.split(jax.random.fold_in(arg_keys[1], 1), TOKENS // TOK)
    expert_ids_turns = jax.random.permutation(jax.random.fold_in(arg_keys[1], 3), TOKENS // TOK)
    expert_ids = jax.vmap(lambda own, number: routed_block(jax.random.fold_in(arg_keys[1], 2), own, number, TOK, EXPERTS, 2, CAP, 2))(expert_ids_keys, expert_ids_turns).reshape((TOKENS, 2))
    gate_values = jnp.clip(0.1 + 0.9 * jax.random.uniform(arg_keys[2], (TOKENS, 2), jnp.float32) ** shard_levels(arg_keys[2], (TOKENS, 2), ((0, 32),), -0.2, 0.2), 0.1, 1.0)
    w_gate = bell_draw(arg_keys[3], (D, EXPERTS * HIDDEN_SIZE), D ** -0.5, 0.078125, ((0, 24), (1, 32)))
    w_up = bell_draw(arg_keys[4], (D, EXPERTS * HIDDEN_SIZE), D ** -0.5, 0.078125, ((0, 24), (1, 32)))
    w_down = bell_draw(arg_keys[5], (EXPERTS * HIDDEN_SIZE, D), HIDDEN_SIZE ** -0.5, 0.0625, ((0, 32), (1, 24)))
    scale_gate = jnp.clip(jnp.exp(math.log(2.0) - 1.3862944 * jax.random.uniform(arg_keys[6], (D // BLOCK, EXPERTS * HIDDEN_SIZE // BLOCK), jnp.float32) ** shard_levels(arg_keys[6], (D // BLOCK, EXPERTS * HIDDEN_SIZE // BLOCK), ((0, 24), (1, 32)), -0.2, 0.2)), 0.5, 2.0)
    scale_up = jnp.clip(jnp.exp(math.log(2.0) - 1.3862944 * jax.random.uniform(arg_keys[7], (D // BLOCK, EXPERTS * HIDDEN_SIZE // BLOCK), jnp.float32) ** shard_levels(arg_keys[7], (D // BLOCK, EXPERTS * HIDDEN_SIZE // BLOCK), ((0, 24), (1, 32)), -0.2, 0.2)), 0.5, 2.0)
    scale_down = jnp.clip(jnp.exp(math.log(2.0) - 1.3862944 * jax.random.uniform(arg_keys[8], (EXPERTS * HIDDEN_SIZE // BLOCK, D // BLOCK), jnp.float32) ** shard_levels(arg_keys[8], (EXPERTS * HIDDEN_SIZE // BLOCK, D // BLOCK), ((0, 32), (1, 24)), -0.2, 0.2)), 0.5, 2.0)
    return dict(tokens=tokens, expert_ids=expert_ids, gate_values=gate_values, w_gate=w_gate, w_up=w_up, w_down=w_down, scale_gate=scale_gate, scale_up=scale_up, scale_down=scale_down)


def rounded(values):
    return lax.optimization_barrier(values.astype(jnp.bfloat16)).astype(jnp.float32)


def dequant(weights, block_scale):
    spread = jnp.repeat(jnp.repeat(block_scale, BLOCK, axis=0), BLOCK, axis=1)
    return (weights.astype(jnp.float32) * spread.astype(jnp.float32)).astype(jnp.bfloat16)


def reference(tokens, expert_ids, gate_values, w_gate, w_up, w_down, scale_gate, scale_up, scale_down):
    slices = N_EXPERT // EXPERTS
    feature_width = D // N_FSDP
    slice_width = HIDDEN_SIZE // slices
    buffer_rows = N_EXPERT * CAP
    scale_cols = HIDDEN_SIZE // BLOCK
    flat_ids = expert_ids.reshape(-1).astype(jnp.int32)
    owners = jnp.repeat(jnp.arange(TOKENS, dtype=jnp.int32), 2)
    onehot = (flat_ids[:, None] == jnp.arange(EXPERTS, dtype=jnp.int32)[None, :]).astype(jnp.int32)
    slot_rank = jnp.sum((jnp.cumsum(onehot, axis=0) - onehot) * onehot, axis=1).astype(jnp.int32)
    buffers = jnp.zeros((EXPERTS, buffer_rows, D), jnp.bfloat16).at[flat_ids, slot_rank].set(tokens[owners])

    def expert_out(expert_index):
        rows_in = buffers[expert_index]
        col_start = expert_index * HIDDEN_SIZE
        scale_start = expert_index * scale_cols
        gate_deq = dequant(lax.dynamic_slice_in_dim(w_gate, col_start, HIDDEN_SIZE, 1),
                           lax.dynamic_slice_in_dim(scale_gate, scale_start, scale_cols, 1))
        up_deq = dequant(lax.dynamic_slice_in_dim(w_up, col_start, HIDDEN_SIZE, 1),
                         lax.dynamic_slice_in_dim(scale_up, scale_start, scale_cols, 1))
        down_deq = dequant(lax.dynamic_slice_in_dim(w_down, col_start, HIDDEN_SIZE, 0),
                           lax.dynamic_slice_in_dim(scale_down, scale_start, scale_cols, 0))
        gate_sum = jnp.zeros((buffer_rows, HIDDEN_SIZE), jnp.float32)
        up_sum = jnp.zeros((buffer_rows, HIDDEN_SIZE), jnp.float32)
        for block_index in range(N_FSDP):
            low_edge = block_index * feature_width
            high_edge = low_edge + feature_width
            gate_sum = gate_sum + rounded(jnp.dot(rows_in[:, low_edge:high_edge], gate_deq[low_edge:high_edge], preferred_element_type=jnp.float32))
            up_sum = up_sum + rounded(jnp.dot(rows_in[:, low_edge:high_edge], up_deq[low_edge:high_edge], preferred_element_type=jnp.float32))
        hidden = (jax.nn.silu(gate_sum) * up_sum).astype(jnp.bfloat16)
        output = jnp.zeros((buffer_rows, D), jnp.float32)
        for slice_index in range(slices):
            low_edge = slice_index * slice_width
            high_edge = low_edge + slice_width
            output = output + rounded(jnp.dot(hidden[:, low_edge:high_edge], down_deq[low_edge:high_edge], preferred_element_type=jnp.float32))
        return output

    per_expert = lax.map(expert_out, jnp.arange(EXPERTS, dtype=jnp.int32))
    per_assign = per_expert[flat_ids, slot_rank]
    weighted = per_assign * gate_values.reshape(-1)[:, None].astype(jnp.float32)
    return jnp.sum(weighted.reshape(TOKENS, 2, D), axis=1).astype(jnp.bfloat16)
```

```python
import functools

import jax
import jax.numpy as jnp
from jax import lax
from jax.experimental import pallas as pl
from jax.experimental.pallas import tpu as pltpu
from jax.sharding import PartitionSpec as P

EXPERTS = 8
BLOCK = 128
CAP = 24
PIECES = 4
OFFSETS = (0, 1, 2, 3)
MESH = pl.DeviceIdType.MESH


def schedule(half):
    tasks = []
    for piece in range(PIECES):
        begin = OFFSETS[piece]
        tasks.append((begin - 0.5, 0, "mul", piece, 0))
        for hop in range(half, 0, -1):
            tasks.append((begin + half - hop, 1, "sum", piece, hop))
        tasks.append((begin + half, 2, "act", piece, 0))
    for part in range(2):
        begin = max(OFFSETS[2 * part], OFFSETS[2 * part + 1]) + half
        for hop in range(1, half + 1):
            tasks.append((begin + hop - 0.5, 3, "gather", part, hop))
    begin = max(OFFSETS) + half
    tasks.append((begin + 0.6, 4, "down", 0, 0))
    for hop in range(1, half + 1):
        tasks.append((begin + hop + 0.6, 4, "down", 0, hop))
    return sorted(tasks)


def expert_kernel(
    ring,
    x_ref,
    wg_ref,
    wu_ref,
    wd_ref,
    sg_ref,
    su_ref,
    sd_ref,
    out_ref,
    x_all,
    w_send,
    w_all,
    d_send,
    d_own,
    d_far,
    parts,
    sum_out,
    sum_in,
    hidden,
    y_own,
    y_out,
    y_in,
    x_sems,
    w_sems,
    sum_sems,
    gather_sems,
    y_sems,
):
    half = ring // 2
    width = x_ref.shape[1]
    rows = x_ref.shape[0]
    chunk = rows // ring
    units = wg_ref.shape[1] // 2
    cols = units // PIECES
    place = lax.axis_index("fsdp")
    z = place // 2
    side = place % 2
    mate = {"fsdp": z * 2 + (1 - side)}
    step = {
        0: {"fsdp": ((z + 1) % ring) * 2 + side},
        1: {"fsdp": ((z + ring - 1) % ring) * 2 + side},
    }
    sends = []

    def remote(src, dst, sems, index, target):
        return pltpu.make_async_remote_copy(
            src_ref=src,
            dst_ref=dst,
            send_sem=sems.at[(0,) + index],
            recv_sem=sems.at[(1,) + index],
            device_id=target,
            device_id_type=MESH,
        )

    def send(*args):
        copy = remote(*args)
        copy.start()
        sends.append(copy)

    barrier = pltpu.get_barrier_semaphore()
    for target in (mate, step[0], step[1]):
        pl.semaphore_signal(barrier, inc=1, device_id=target, device_id_type=MESH)

    def scaled(w_ref, s_ref, block, start):
        start = pl.multiple_of(start, cols)
        values = w_ref[block * BLOCK : (block + 1) * BLOCK, pl.ds(start, cols)]
        return (values.astype(jnp.float32) * s_ref[block : block + 1, pl.ds(start, cols)]).astype(
            jnp.bfloat16
        )

    def fill(dst, piece, owner):
        for block in range(width // BLOCK):
            low = block * BLOCK
            start = owner * units + piece * cols
            dst[piece, low : low + BLOCK, :cols] = scaled(wg_ref, sg_ref, block, start)
            dst[piece, low : low + BLOCK, cols:] = scaled(wu_ref, su_ref, block, start)

    def fill_down(dst, owner):
        for block in range(units // BLOCK):
            start = pl.multiple_of(owner * units + block * BLOCK, BLOCK)
            row = sd_ref[pl.ds(owner * (units // BLOCK) + block, 1), :]
            values = wd_ref[pl.ds(start, BLOCK), :].astype(jnp.float32) * row
            dst[block * BLOCK : (block + 1) * BLOCK, :] = values.astype(jnp.bfloat16)

    for piece in range(PIECES):
        fill(w_send, piece, 1 - side)
    pl.semaphore_wait(barrier, 3)
    send(x_ref, x_all.at[:, width:], x_sems, (0,), mate)
    for piece in range(PIECES):
        send(w_send.at[piece], w_all.at[piece, width:, :], w_sems, (piece,), mate)
    fill_down(d_send, 1 - side)
    send(d_send, d_far, w_sems, (PIECES,), mate)
    x_all[:, :width] = x_ref[...]
    for piece in range(PIECES):
        fill(w_all, piece, side)
    fill_down(d_own, side)
    remote(x_ref, x_all.at[:, width:], x_sems, (0,), mate).wait_recv()

    def rows_of(index):
        return pl.ds(pl.multiple_of(index * chunk, chunk), chunk)

    def runs(way, piece, hop):
        return 1 <= hop < half or (hop == half and piece // (PIECES // 2) == way)

    def wait_sum(way, hop, piece):
        remote(
            sum_out.at[way, hop - 1, piece],
            sum_in.at[way, hop - 1, piece],
            sum_sems,
            (way, hop - 1, piece),
            step[way],
        ).wait_recv()

    def wait_hidden(way, hop, part):
        origin = (z + ring - hop) % ring if way == 0 else (z + hop) % ring
        remote(
            hidden.at[origin, part],
            hidden.at[origin, part],
            gather_sems,
            (way, hop - 1, part),
            step[way],
        ).wait_recv()

    def gathers(way, part, hop):
        return 1 <= hop < half or (hop == half and part == way)

    arrived = set()

    def ready(way, hop, part):
        if (way, hop, part) not in arrived:
            arrived.add((way, hop, part))
            wait_hidden(way, hop, part)

    row_tile = rows // 3
    for _, _, kind, first, hop in schedule(half):
        if kind == "mul":
            piece = first
            remote(
                w_send.at[piece], w_all.at[piece, width:, :], w_sems, (piece,), mate
            ).wait_recv()
            for tile in range(3):
                low = tile * row_tile
                parts[piece, low : low + row_tile, :] = jnp.dot(
                    x_all[low : low + row_tile, :],
                    w_all[piece],
                    preferred_element_type=jnp.float32,
                )
        elif kind == "sum":
            piece = first
            for way in range(2):
                if not runs(way, piece, hop):
                    continue
                owner = (z + hop) % ring if way == 0 else (z + ring - hop) % ring
                total = parts[piece, rows_of(owner), :]
                if runs(way, piece, hop + 1):
                    wait_sum(way, hop + 1, piece)
                    total = total + sum_in[way, hop, piece].astype(jnp.float32)
                sum_out[way, hop - 1, piece] = total.astype(jnp.bfloat16)
                send(
                    sum_out.at[way, hop - 1, piece],
                    sum_in.at[way, hop - 1, piece],
                    sum_sems,
                    (way, hop - 1, piece),
                    step[way],
                )
        elif kind == "act":
            piece = first
            total = parts[piece, rows_of(z), :]
            for way in range(2):
                wait_sum(way, 1, piece)
                total = total + sum_in[way, 0, piece].astype(jnp.float32)
            gate = total[:, :cols]
            act = gate / (1.0 + jnp.exp(-gate)) * total[:, cols:]
            low = (piece % 2) * cols
            hidden[z, piece // 2, :, low : low + cols] = act.astype(jnp.bfloat16)
        elif kind == "gather":
            part = first
            for way in range(2):
                if not gathers(way, part, hop):
                    continue
                if hop > 1:
                    ready(way, hop - 1, part)
                origin = (z + ring - hop + 1) % ring if way == 0 else (z + hop - 1) % ring
                send(
                    hidden.at[origin, part],
                    hidden.at[origin, part],
                    gather_sems,
                    (way, hop - 1, part),
                    step[way],
                )
        else:
            if hop == 0:
                remote(d_send, d_far, w_sems, (PIECES,), mate).wait_recv()
                todo = ((0, z),)
            elif hop < half:
                todo = ((2 * hop - 1, (z + ring - hop) % ring), (2 * hop, (z + hop) % ring))
            else:
                todo = ((ring - 1, (z + half) % ring),)
            if hop > 0:
                for way in range(2):
                    for part in range(2):
                        if gathers(way, part, hop):
                            ready(way, hop, part)
            for slot, origin in todo:
                own = jnp.zeros((chunk, width), jnp.float32)
                far = jnp.zeros((chunk, width), jnp.float32)
                for part in range(2):
                    low = part * (units // 2)
                    lhs = hidden[origin, part]
                    own = own + jnp.dot(
                        lhs, d_own[low : low + units // 2, :], preferred_element_type=jnp.float32
                    )
                    far = far + jnp.dot(
                        lhs, d_far[low : low + units // 2, :], preferred_element_type=jnp.float32
                    )
                y_own[slot] = own
                y_out[slot] = far.astype(jnp.bfloat16)
                send(y_out.at[slot], y_in.at[slot], y_sems, (slot,), mate)

    for slot in range(ring):
        if slot == 0:
            origin = z
        elif slot == ring - 1:
            origin = (z + half) % ring
        elif slot % 2 == 1:
            origin = (z + ring - (slot + 1) // 2) % ring
        else:
            origin = (z + slot // 2) % ring
        remote(y_out.at[slot], y_in.at[slot], y_sems, (slot,), mate).wait_recv()
        out_ref[rows_of(origin), :] = (
            y_own[slot] + y_in[slot].astype(jnp.float32)
        ).astype(jnp.bfloat16)
    for copy in sends:
        copy.wait_send()


def expert_call(incoming, w_gate, w_up, w_down, s_gate, s_up, s_down, ring):
    rows, width = incoming.shape
    units = w_gate.shape[1] // 2
    cols = units // PIECES
    half = ring // 2
    chunk = rows // ring
    vmem = pl.BlockSpec(memory_space=pltpu.VMEM)
    bf16, f32 = jnp.bfloat16, jnp.float32
    return pl.pallas_call(
        functools.partial(expert_kernel, ring),
        out_shape=jax.ShapeDtypeStruct((rows, width), bf16),
        in_specs=[vmem] * 7,
        out_specs=vmem,
        scratch_shapes=[
            pltpu.VMEM((rows, 2 * width), bf16),
            pltpu.VMEM((PIECES, width, 2 * cols), bf16),
            pltpu.VMEM((PIECES, 2 * width, 2 * cols), bf16),
            pltpu.VMEM((units, width), bf16),
            pltpu.VMEM((units, width), bf16),
            pltpu.VMEM((units, width), bf16),
            pltpu.VMEM((PIECES, rows, 2 * cols), f32),
            pltpu.VMEM((2, half, PIECES, chunk, 2 * cols), bf16),
            pltpu.VMEM((2, half, PIECES, chunk, 2 * cols), bf16),
            pltpu.VMEM((ring, 2, chunk, units // 2), bf16),
            pltpu.VMEM((ring, chunk, width), f32),
            pltpu.VMEM((ring, chunk, width), bf16),
            pltpu.VMEM((ring, chunk, width), bf16),
            pltpu.SemaphoreType.DMA((2, 1)),
            pltpu.SemaphoreType.DMA((2, PIECES + 1)),
            pltpu.SemaphoreType.DMA((2, 2, half, PIECES)),
            pltpu.SemaphoreType.DMA((2, 2, half, 2)),
            pltpu.SemaphoreType.DMA((2, ring)),
        ],
        compiler_params=pltpu.CompilerParams(collective_id=0, has_side_effects=True),
        name="expert_layer",
    )(incoming, w_gate, w_up, w_down, s_gate, s_up, s_down)


def shards(tokens, expert_ids, gate_values, w_gate, w_up, w_down, scale_gate, scale_up, scale_down):
    device_count = lax.axis_size("expert")
    ring = lax.axis_size("fsdp") // 2
    slices = device_count // EXPERTS
    local_tokens = tokens.shape[0]
    feature_cols = tokens.shape[1]
    slot_total = EXPERTS * CAP
    flat_ids = expert_ids.reshape(-1)
    onehot = (flat_ids[:, None] == jnp.arange(EXPERTS, dtype=jnp.int32)[None, :]).astype(jnp.int32)
    slot_rank = jnp.sum((jnp.cumsum(onehot, axis=0) - onehot) * onehot, axis=1)
    target = flat_ids * CAP + slot_rank
    placing = (target[:, None] == jnp.arange(slot_total, dtype=jnp.int32)[None, :]).astype(
        jnp.float32
    )
    token_map = jnp.sum(placing.reshape(local_tokens, 2, slot_total), axis=1).astype(jnp.bfloat16)
    packed = jnp.einsum("ts,td->sd", token_map, tokens, preferred_element_type=jnp.float32).astype(
        jnp.bfloat16
    )
    outgoing = jnp.broadcast_to(
        packed.reshape(EXPERTS, 1, CAP, feature_cols), (EXPERTS, slices, CAP, feature_cols)
    ).reshape(device_count * CAP, feature_cols)
    incoming = lax.all_to_all(outgoing, "expert", split_axis=0, concat_axis=0, tiled=True)
    partial_rows = expert_call(
        incoming,
        w_gate,
        w_up,
        w_down,
        jnp.repeat(scale_gate, BLOCK, axis=1),
        jnp.repeat(scale_up, BLOCK, axis=1),
        jnp.repeat(scale_down, BLOCK, axis=1),
        ring,
    )
    returned = lax.all_to_all(partial_rows, "expert", split_axis=0, concat_axis=0, tiled=True)
    slice_sums = jnp.sum(
        returned.reshape(EXPERTS, slices, CAP, feature_cols).astype(jnp.float32), axis=1
    )
    slice_sums = slice_sums.reshape(slot_total, feature_cols)
    weights_map = jnp.sum(
        (placing * gate_values.reshape(-1)[:, None]).reshape(local_tokens, 2, slot_total), axis=1
    )
    mixed_rows = jnp.dot(
        weights_map, slice_sums, precision=lax.Precision.HIGHEST, preferred_element_type=jnp.float32
    )
    return mixed_rows.astype(jnp.bfloat16)


def solution(mesh):
    in_specs = (
        P("expert", "fsdp"),
        P("expert", None),
        P("expert", None),
        P("fsdp", "expert"),
        P("fsdp", "expert"),
        P("expert", "fsdp"),
        P("fsdp", "expert"),
        P("fsdp", "expert"),
        P("expert", "fsdp"),
    )
    out_specs = P("expert", "fsdp")
    return jax.shard_map(shards, mesh=mesh, in_specs=in_specs, out_specs=out_specs, check_vma=False)
```

```python
import functools

import jax
import jax.numpy as jnp
from jax import lax
from jax.experimental import pallas as pl
from jax.experimental.pallas import tpu as pltpu
from jax.sharding import PartitionSpec as P

EXPERTS = 8
BLOCK = 128
CAP = 24
PIECES = 4
OFFSETS = (0, 0, 2, 4)
MESH = pl.DeviceIdType.MESH


def schedule(half):
    tasks = []
    for piece in range(PIECES):
        begin = OFFSETS[piece]
        tasks.append((begin - 0.5, 0, "mul", piece, 0))
        for hop in range(half, 0, -1):
            tasks.append((begin + half - hop, 1, "sum", piece, hop))
        tasks.append((begin + half, 2, "act", piece, 0))
    for part in range(2):
        begin = max(OFFSETS[2 * part], OFFSETS[2 * part + 1]) + half
        for hop in range(1, half + 1):
            tasks.append((begin + hop - 0.5, 3, "gather", part, hop))
    begin = max(OFFSETS) + half
    tasks.append((begin + 0.6, 4, "down", 0, 0))
    for hop in range(1, half + 1):
        tasks.append((begin + hop + 0.6, 4, "down", 0, hop))
    for hop in range(half + 1):
        tasks.append((begin + hop + 1.7, 5, "back", 0, hop))
    return sorted(tasks)


def expert_kernel(
    ring,
    idc_ref,
    idr_ref,
    gv_ref,
    tok_ref,
    wg_ref,
    wu_ref,
    wd_ref,
    sg_ref,
    su_ref,
    sd_ref,
    out_ref,
    packed,
    x_near,
    x_far,
    x_all,
    w_send,
    w_all,
    d_send,
    d_own,
    d_far,
    parts,
    sum_out,
    sum_in,
    hidden,
    y_own,
    y_out,
    y_in,
    y_back,
    landed,
    route_sems,
    mate_sems,
    near_sems,
    far_sems,
    w_sems,
    sum_sems,
    gather_sems,
    y_sems,
    back_sems,
):
    half = ring // 2
    local_tokens, width = tok_ref.shape
    rows = x_all.shape[0]
    chunk = rows // ring
    units = wg_ref.shape[1] // 2
    cols = units // PIECES
    slots = EXPERTS * CAP
    place = lax.axis_index("fsdp")
    z = place // 2
    side = place % 2
    seat = lax.axis_index("expert")
    high = seat // 16
    y = (seat // 2) % 8
    core = seat % 2
    expert = high * 4 + y // 2
    share = (y % 2) * 2 + core
    mate = {"fsdp": z * 2 + (1 - side)}
    sibling = {"expert": seat + 1 - 2 * core}
    step = {
        0: {"fsdp": ((z + 1) % ring) * 2 + side},
        1: {"fsdp": ((z + ring - 1) % ring) * 2 + side},
    }
    sends = []

    def remote(src, dst, sems, index, target):
        return pltpu.make_async_remote_copy(
            src_ref=src,
            dst_ref=dst,
            send_sem=sems.at[(0,) + index],
            recv_sem=sems.at[(1,) + index],
            device_id=target,
            device_id_type=MESH,
        )

    def send(*args):
        copy = remote(*args)
        copy.start()
        sends.append(copy)

    barrier = pltpu.get_barrier_semaphore()
    for target in (mate, step[0], step[1]):
        pl.semaphore_signal(barrier, inc=1, device_id=target, device_id_type=MESH)
    for other in range(1, 32):
        target = {"expert": (seat + other) % 32}
        pl.semaphore_signal(barrier, inc=1, device_id=target, device_id_type=MESH)

    def scaled(w_ref, s_ref, block, start):
        tiles = []
        for lane in range(cols // BLOCK):
            low = pl.multiple_of(start + lane * BLOCK, BLOCK)
            values = w_ref[block * BLOCK : (block + 1) * BLOCK, pl.ds(low, BLOCK)]
            scale = s_ref[block, start // BLOCK + lane]
            tiles.append((values.astype(jnp.float32) * scale).astype(jnp.bfloat16))
        return tiles

    def fill(dst, piece, owner):
        for block in range(width // BLOCK):
            low = block * BLOCK
            start = owner * units + piece * cols
            for index, (w_ref, s_ref) in enumerate(((wg_ref, sg_ref), (wu_ref, su_ref))):
                for lane, tile in enumerate(scaled(w_ref, s_ref, block, start)):
                    left = index * cols + lane * BLOCK
                    dst[piece, low : low + BLOCK, left : left + BLOCK] = tile

    def fill_down(dst, owner):
        for block in range(units // BLOCK):
            start = pl.multiple_of(owner * units + block * BLOCK, BLOCK)
            for lane in range(width // BLOCK):
                left = lane * BLOCK
                scale = sd_ref[owner * (units // BLOCK) + block, lane]
                values = wd_ref[pl.ds(start, BLOCK), left : left + BLOCK].astype(jnp.float32)
                dst[block * BLOCK : (block + 1) * BLOCK, left : left + BLOCK] = (
                    values * scale
                ).astype(jnp.bfloat16)

    def iota(shape, axis):
        return lax.broadcasted_iota(jnp.int32, shape, axis)

    def mask(test, kind):
        return jnp.where(test, 1.0, 0.0).astype(kind)

    square = (local_tokens, local_tokens)
    names = iota((EXPERTS, local_tokens), 0)
    picks = [mask(names == idr_ref[k : k + 1, :], jnp.float32) for k in range(2)]
    before = jnp.dot(
        (picks[0] + picks[1]).astype(jnp.bfloat16),
        mask(iota(square, 0) < iota(square, 1), jnp.bfloat16),
        preferred_element_type=jnp.float32,
    )
    spots = iota((slots, local_tokens), 0)
    chosen = jnp.zeros((slots, local_tokens), jnp.float32)
    for k in range(2):
        rank = jnp.sum(before * picks[k], axis=0, keepdims=True).astype(jnp.int32)
        chosen = chosen + mask(spots == idr_ref[k : k + 1, :] * CAP + rank, jnp.float32)
    picked = jnp.dot(
        chosen.astype(jnp.bfloat16), tok_ref[...], preferred_element_type=jnp.float32
    )
    packed[...] = picked.reshape(packed.shape).astype(jnp.bfloat16)

    fill(w_send, 0, 1 - side)
    pl.semaphore_wait(barrier, 34)
    my_block = core * 2 + high

    def block_of(turn):
        return core * 2 + (high + turn) % 2

    def send_piece(piece):
        send(w_send.at[piece], w_all.at[piece, width:, :], w_sems, (piece,), mate)

    def wait_bytes(ref, sem):
        pltpu.make_async_copy(ref, ref, sem).wait()

    for turn in range(2):
        for other in (4, 3, 5, 2, 6, 1, 7, 0):
            to_high = (high + turn) % 2
            to_y = (y + other) % 8
            src = packed.at[to_high * 4 + to_y // 2]
            dst = x_near.at[my_block, :, y]
            if turn == 0 and other == 0:
                pltpu.make_async_copy(src, dst, route_sems.at[1, 0]).start()
            else:
                target = {"expert": to_high * 16 + to_y * 2 + core}
                remote(src, dst, route_sems, (turn,), target).start()
    send_piece(0)
    for piece in range(1, PIECES):
        fill(w_send, piece, 1 - side)
    for piece in range(PIECES):
        fill(w_all, piece, side)
    for turn in range(2):
        block = block_of(turn)
        wait_bytes(x_near.at[block], route_sems.at[1, turn])
        send(x_near.at[block], x_far.at[block], mate_sems, (turn,), mate)
        send(x_near.at[block], x_near.at[block], near_sems, (turn,), sibling)
    for piece in range(1, PIECES):
        send_piece(piece)
    fill_down(d_send, 1 - side)
    send(d_send, d_far, w_sems, (PIECES,), mate)
    for turn in range(2):
        block = block_of(turn)
        remote(x_near.at[block], x_far.at[block], mate_sems, (turn,), mate).wait_recv()
        send(x_far.at[block], x_far.at[block], far_sems, (turn,), sibling)
    fill_down(d_own, side)
    for turn in range(2):
        block = (1 - core) * 2 + (high + turn) % 2
        remote(x_near.at[block], x_near.at[block], near_sems, (turn,), sibling).wait_recv()
        remote(x_far.at[block], x_far.at[block], far_sems, (turn,), sibling).wait_recv()
    part_rows = rows // 4
    for block in range(4):
        for index, source in enumerate((x_near, x_far)):
            values = source[block].astype(jnp.float32).reshape(part_rows, width)
            x_all[
                block * part_rows : (block + 1) * part_rows, index * width : (index + 1) * width
            ] = values.astype(jnp.bfloat16)

    def rows_of(index):
        return pl.ds(pl.multiple_of(index * chunk, chunk), chunk)

    def runs(way, piece, hop):
        return 1 <= hop < half or (hop == half and piece // (PIECES // 2) == way)

    def wait_sum(way, hop, piece):
        remote(
            sum_out.at[way, hop - 1, piece],
            sum_in.at[way, hop - 1, piece],
            sum_sems,
            (way, hop - 1, piece),
            step[way],
        ).wait_recv()

    def wait_hidden(way, hop, part):
        origin = (z + ring - hop) % ring if way == 0 else (z + hop) % ring
        remote(
            hidden.at[origin, part],
            hidden.at[origin, part],
            gather_sems,
            (way, hop - 1, part),
            step[way],
        ).wait_recv()

    def gathers(way, part, hop):
        return 1 <= hop < half or (hop == half and part == way)

    arrived = set()

    def ready(way, hop, part):
        if (way, hop, part) not in arrived:
            arrived.add((way, hop, part))
            wait_hidden(way, hop, part)

    def chunks_at(hop):
        if hop == 0:
            return ((0, z),)
        if hop < half:
            return ((2 * hop - 1, (z + ring - hop) % ring), (2 * hop, (z + hop) % ring))
        return ((ring - 1, (z + half) % ring),)

    row_tile = rows // 3
    for _, _, kind, first, hop in schedule(half):
        if kind == "mul":
            piece = first
            remote(
                w_send.at[piece], w_all.at[piece, width:, :], w_sems, (piece,), mate
            ).wait_recv()
            for tile in range(3):
                low = tile * row_tile
                parts[piece, low : low + row_tile, :] = jnp.dot(
                    x_all[low : low + row_tile, :],
                    w_all[piece],
                    preferred_element_type=jnp.float32,
                )
        elif kind == "sum":
            piece = first
            for way in range(2):
                if not runs(way, piece, hop):
                    continue
                owner = (z + hop) % ring if way == 0 else (z + ring - hop) % ring
                total = parts[piece, rows_of(owner), :]
                if runs(way, piece, hop + 1):
                    wait_sum(way, hop + 1, piece)
                    total = total + sum_in[way, hop, piece].astype(jnp.float32)
                sum_out[way, hop - 1, piece] = total.astype(jnp.bfloat16)
                send(
                    sum_out.at[way, hop - 1, piece],
                    sum_in.at[way, hop - 1, piece],
                    sum_sems,
                    (way, hop - 1, piece),
                    step[way],
                )
        elif kind == "act":
            piece = first
            total = parts[piece, rows_of(z), :]
            for way in range(2):
                wait_sum(way, 1, piece)
                total = total + sum_in[way, 0, piece].astype(jnp.float32)
            gate = total[:, :cols]
            act = gate / (1.0 + jnp.exp(-gate)) * total[:, cols:]
            low = (piece % 2) * cols
            hidden[z, piece // 2, :, low : low + cols] = act.astype(jnp.bfloat16)
        elif kind == "gather":
            part = first
            for way in range(2):
                if not gathers(way, part, hop):
                    continue
                if hop > 1:
                    ready(way, hop - 1, part)
                origin = (z + ring - hop + 1) % ring if way == 0 else (z + hop - 1) % ring
                send(
                    hidden.at[origin, part],
                    hidden.at[origin, part],
                    gather_sems,
                    (way, hop - 1, part),
                    step[way],
                )
        elif kind == "down":
            if hop == 0:
                remote(d_send, d_far, w_sems, (PIECES,), mate).wait_recv()
            else:
                for way in range(2):
                    for part in range(2):
                        if gathers(way, part, hop):
                            ready(way, hop, part)
            for slot, origin in chunks_at(hop):
                own = jnp.zeros((chunk, width), jnp.float32)
                far = jnp.zeros((chunk, width), jnp.float32)
                for part in range(2):
                    low = part * (units // 2)
                    lhs = hidden[origin, part]
                    far = far + jnp.dot(
                        lhs, d_far[low : low + units // 2, :], preferred_element_type=jnp.float32
                    )
                    own = own + jnp.dot(
                        lhs, d_own[low : low + units // 2, :], preferred_element_type=jnp.float32
                    )
                y_own[slot] = own
                y_out[slot] = far.astype(jnp.bfloat16)
                send(y_out.at[slot], y_in.at[slot], y_sems, (slot,), mate)
        else:
            for slot, origin in chunks_at(hop):
                remote(y_out.at[slot], y_in.at[slot], y_sems, (slot,), mate).wait_recv()
                total = y_own[slot] + y_in[slot].astype(jnp.float32)
                y_back[slot * 8 : slot * 8 + 8] = total.reshape(8, 8, width).astype(jnp.bfloat16)
                block = origin // 3
                dst = landed.at[share, expert, origin % 3]
                for other in range(8):
                    to_y = (y + other) % 8
                    src = y_back.at[slot * 8 + to_y]
                    target = {"expert": (block % 2) * 16 + to_y * 2 + block // 2}
                    copy = remote(src, dst, back_sems, (), target)
                    if other > 0:
                        copy.start()
                    else:
                        pl.when(block != my_block)(copy.start)
                        pl.when(block == my_block)(
                            pltpu.make_async_copy(src, dst, back_sems.at[1]).start
                        )

    lanes = iota((local_tokens, BLOCK), 1)
    picks = [mask(lanes == idc_ref[:, k : k + 1], jnp.float32) for k in range(2)]
    before = jnp.dot(
        mask(iota(square, 1) < iota(square, 0), jnp.bfloat16),
        (picks[0] + picks[1]).astype(jnp.bfloat16),
        preferred_element_type=jnp.float32,
    )
    spots = iota((local_tokens, slots), 1)
    mixing = jnp.zeros((local_tokens, slots), jnp.float32)
    for k in range(2):
        rank = jnp.sum(before * picks[k], axis=1, keepdims=True).astype(jnp.int32)
        found = spots == idc_ref[:, k : k + 1] * CAP + rank
        mixing = mixing + jnp.where(found, gv_ref[:, k : k + 1], 0.0)
    wait_bytes(landed, back_sems.at[1])
    sums = landed[0].astype(jnp.float32)
    for index in range(1, 4):
        sums = sums + landed[index].astype(jnp.float32)
    out_ref[...] = jnp.dot(
        mixing,
        sums.reshape(slots, width),
        precision=lax.Precision.HIGHEST,
        preferred_element_type=jnp.float32,
    ).astype(jnp.bfloat16)

    wait_bytes(packed.at[:7], route_sems.at[0, 0])
    wait_bytes(packed, route_sems.at[0, 1])
    wait_bytes(y_back.at[:93], back_sems.at[0])
    for copy in sends:
        copy.wait_send()


def shards(tokens, expert_ids, gate_values, w_gate, w_up, w_down, scale_gate, scale_up, scale_down):
    ring = lax.axis_size("fsdp") // 2
    local_tokens, width = tokens.shape
    rows = lax.axis_size("expert") * CAP
    units = w_gate.shape[1] // 2
    cols = units // PIECES
    half = ring // 2
    chunk = rows // ring
    vmem = pl.BlockSpec(memory_space=pltpu.VMEM)
    smem = pl.BlockSpec(memory_space=pltpu.SMEM)
    bf16, f32 = jnp.bfloat16, jnp.float32
    dma = pltpu.SemaphoreType.DMA
    return pl.pallas_call(
        functools.partial(expert_kernel, ring),
        out_shape=jax.ShapeDtypeStruct((local_tokens, width), bf16),
        in_specs=[vmem] * 7 + [smem] * 3,
        out_specs=vmem,
        scratch_shapes=[
            pltpu.VMEM((EXPERTS, 3, 8, width), bf16),
            pltpu.VMEM((4, 3, 8, 8, width), bf16),
            pltpu.VMEM((4, 3, 8, 8, width), bf16),
            pltpu.VMEM((rows, 2 * width), bf16),
            pltpu.VMEM((PIECES, width, 2 * cols), bf16),
            pltpu.VMEM((PIECES, 2 * width, 2 * cols), bf16),
            pltpu.VMEM((units, width), bf16),
            pltpu.VMEM((units, width), bf16),
            pltpu.VMEM((units, width), bf16),
            pltpu.VMEM((PIECES, rows, 2 * cols), f32),
            pltpu.VMEM((2, half, PIECES, chunk, 2 * cols), bf16),
            pltpu.VMEM((2, half, PIECES, chunk, 2 * cols), bf16),
            pltpu.VMEM((ring, 2, chunk, units // 2), bf16),
            pltpu.VMEM((ring, chunk, width), f32),
            pltpu.VMEM((ring, chunk, width), bf16),
            pltpu.VMEM((ring, chunk, width), bf16),
            pltpu.VMEM((ring * 8, 8, width), bf16),
            pltpu.VMEM((4, EXPERTS, 3, 8, width), bf16),
            dma((2, 2)),
            dma((2, 2)),
            dma((2, 2)),
            dma((2, 2)),
            dma((2, PIECES + 1)),
            dma((2, 2, half, PIECES)),
            dma((2, 2, half, 2)),
            dma((2, ring)),
            dma((2,)),
        ],
        compiler_params=pltpu.CompilerParams(collective_id=0, has_side_effects=True),
        name="expert_layer",
    )(
        expert_ids,
        expert_ids.T,
        gate_values,
        tokens,
        w_gate,
        w_up,
        w_down,
        scale_gate,
        scale_up,
        scale_down,
    )


def solution(mesh):
    in_specs = (
        P("expert", "fsdp"),
        P("expert", None),
        P("expert", None),
        P("fsdp", "expert"),
        P("fsdp", "expert"),
        P("expert", "fsdp"),
        P("fsdp", "expert"),
        P("fsdp", "expert"),
        P("expert", "fsdp"),
    )
    out_specs = P("expert", "fsdp")
    return jax.shard_map(shards, mesh=mesh, in_specs=in_specs, out_specs=out_specs, check_vma=False)
```

```python
import functools

import jax
import jax.numpy as jnp
from jax import lax
from jax.experimental import pallas as pl
from jax.experimental.pallas import tpu as pltpu
from jax.sharding import PartitionSpec as P

EXPERTS = 8
BLOCK = 128
CAP = 24
PIECES = 8
PARTS = 4
FIRST = 2
X_AT = 19.0
W_AT = (8.0, 11.0, 18.5, 21.5, 24.5, 27.5, 30.5, 33.5)
D_AT = 45.5
COPY_LAG = 1.6
CHUNK_TIME = 5.8
MESH = pl.DeviceIdType.MESH


def runs(way, piece, hop, half):
    return 1 <= hop < half or (hop == half and piece // (PIECES // 2) == way)


def gathers(way, part, hop, half):
    return 1 <= hop < half or (hop == half and part // (PARTS // 2) == way)


def sources_of(slot, half):
    if slot == 0:
        return []
    if slot == 2 * half - 1:
        return [("gather", part, half, part // (PARTS // 2)) for part in range(PARTS)]
    hop, way = (slot + 1) // 2, (slot + 1) % 2
    return [("gather", part, hop, way) for part in range(PARTS)]


def schedule(half):
    ways, hops = (0, 1), range(1, half + 1)
    cost = dict(mul=0.45, sum=0.12, act=0.2, gather=0.05, down=0.9, back=0.35)
    rank = dict(gather=1, act=1, sum=1, mul=2, back=3, down=4)
    left = [("mul", piece, 0, 0) for piece in range(PIECES)]
    left += [
        ("sum", piece, hop, way)
        for piece in range(PIECES)
        for hop in hops
        for way in ways
        if runs(way, piece, hop, half)
    ]
    left += [("act", piece, 0, 0) for piece in range(PIECES)]
    left += [
        ("gather", part, hop, way)
        for part in range(PARTS)
        for hop in hops
        for way in ways
        if gathers(way, part, hop, half)
    ]
    left += [(kind, slot, 0, 0) for kind in ("down", "back") for slot in range(2 * half)]
    done, landing = {}, {}

    def ready(task):
        kind, index, hop, way = task
        per = PIECES // PARTS
        if kind == "mul":
            return max(X_AT, W_AT[index])
        if kind == "sum":
            needs = [done.get(("mul", index, 0, 0))]
            if runs(way, index, hop + 1, half):
                needs.append(landing.get(("sum", index, hop + 1, way)))
        elif kind == "act":
            needs = [landing.get(("sum", index, 1, side)) for side in ways]
        elif kind == "gather" and hop == 1:
            needs = [done.get(("act", index * per + k, 0, 0)) for k in range(per)]
        elif kind == "gather":
            needs = [landing.get(("gather", index, hop - 1, way))]
        elif kind == "down" and index == 0:
            needs = [D_AT] + [done.get(("act", piece, 0, 0)) for piece in range(PIECES)]
        elif kind == "down":
            needs = [D_AT] + [landing.get(source) for source in sources_of(index, half)]
        else:
            needs = [landing.get(("down", index, 0, 0))]
        return None if None in needs else max(needs)

    now, links, order = 0.0, {0: 0.0, 1: 0.0, "mate": D_AT}, []
    while left:
        waiting = [(ready(task), task) for task in left]
        waiting = [entry for entry in waiting if entry[0] is not None]
        now = max(now, min(entry[0] for entry in waiting))
        able = [entry for entry in waiting if entry[0] <= now]
        _, task = min(able, key=lambda entry: (rank[entry[1][0]], entry[0], entry[1]))
        left.remove(task)
        order.append(task)
        kind, _, _, way = task
        now += cost[kind]
        done[task] = now
        if kind in ("sum", "gather", "down"):
            link = "mate" if kind == "down" else way
            load = {
                "sum": CHUNK_TIME / PIECES,
                "gather": CHUNK_TIME / 2 / PARTS,
                "down": CHUNK_TIME / 8,
            }
            links[link] = max(links[link], now) + load[kind]
            landing[task] = links[link] + COPY_LAG
    return order


def expert_kernel(
    ring,
    idr_ref,
    gv_ref,
    tok_ref,
    wg_any,
    wu_any,
    wd_any,
    sg_ref,
    su_ref,
    sd_ref,
    out_ref,
    wg_ref,
    wu_ref,
    wd_ref,
    packed,
    mixing,
    x_near,
    x_far,
    x_all,
    w_send,
    w_all,
    d_send,
    d_own,
    d_far,
    parts,
    sum_out,
    sum_in,
    hidden,
    y_own,
    y_out,
    y_in,
    y_back,
    landed,
    route_sems,
    mate_sems,
    near_sems,
    far_sems,
    w_sems,
    sum_sems,
    gather_sems,
    y_sems,
    back_sems,
    load_sems,
):
    half = ring // 2
    local_tokens, width = tok_ref.shape
    rows = x_all.shape[0]
    chunk = rows // ring
    units = wg_ref.shape[1] // 2
    cols = units // PIECES
    slots = EXPERTS * CAP
    place = lax.axis_index("fsdp")
    z = place // 2
    side = place % 2
    seat = lax.axis_index("expert")
    high = seat // 16
    y = (seat // 2) % 8
    core = seat % 2
    expert = high * 4 + y // 2
    share = (y % 2) * 2 + core
    mate = {"fsdp": z * 2 + (1 - side)}
    sibling = {"expert": seat + 1 - 2 * core}
    step = {
        0: {"fsdp": ((z + 1) % ring) * 2 + side},
        1: {"fsdp": ((z + ring - 1) % ring) * 2 + side},
    }
    sends = []

    def remote(src, dst, sems, index, target):
        return pltpu.make_async_remote_copy(
            src_ref=src,
            dst_ref=dst,
            send_sem=sems.at[(0,) + index],
            recv_sem=sems.at[(1,) + index],
            device_id=target,
            device_id_type=MESH,
        )

    def send(*args):
        copy = remote(*args)
        copy.start()
        sends.append(copy)

    loads = [
        pltpu.make_async_copy(src, dst, load_sems.at[index])
        for index, (src, dst) in enumerate(((wg_any, wg_ref), (wu_any, wu_ref), (wd_any, wd_ref)))
    ]
    for load in loads:
        load.start()
    barrier = pltpu.get_barrier_semaphore()
    for target in (mate, step[0], step[1]):
        pl.semaphore_signal(barrier, inc=1, device_id=target, device_id_type=MESH)
    for other in range(1, 32):
        target = {"expert": (seat + other) % 32}
        pl.semaphore_signal(barrier, inc=1, device_id=target, device_id_type=MESH)

    def scaled(w_ref, s_ref, block, start):
        tiles = []
        for lane in range(cols // BLOCK):
            low = pl.multiple_of(start + lane * BLOCK, BLOCK)
            values = w_ref[block * BLOCK : (block + 1) * BLOCK, pl.ds(low, BLOCK)]
            scale = s_ref[block, start // BLOCK + lane]
            tiles.append((values.astype(jnp.float32) * scale).astype(jnp.bfloat16))
        return tiles

    def fill(dst, piece, owner):
        for block in range(width // BLOCK):
            low = block * BLOCK
            start = owner * units + piece * cols
            for index, (w_ref, s_ref) in enumerate(((wg_ref, sg_ref), (wu_ref, su_ref))):
                for lane, tile in enumerate(scaled(w_ref, s_ref, block, start)):
                    left = index * cols + lane * BLOCK
                    dst[piece, low : low + BLOCK, left : left + BLOCK] = tile

    def fill_down(dst, owner):
        for block in range(units // BLOCK):
            start = pl.multiple_of(owner * units + block * BLOCK, BLOCK)
            for lane in range(width // BLOCK):
                left = lane * BLOCK
                scale = sd_ref[lane, owner * (units // BLOCK) + block]
                values = wd_ref[pl.ds(start, BLOCK), left : left + BLOCK].astype(jnp.float32)
                dst[block * BLOCK : (block + 1) * BLOCK, left : left + BLOCK] = (
                    values * scale
                ).astype(jnp.bfloat16)

    def iota(shape, axis):
        return lax.broadcasted_iota(jnp.int32, shape, axis)

    def mask(test, kind):
        return jnp.where(test, 1.0, 0.0).astype(kind)

    square = (local_tokens, local_tokens)
    names = iota((EXPERTS, local_tokens), 0)
    picks = [mask(names == idr_ref[k : k + 1, :], jnp.float32) for k in range(2)]
    before = jnp.dot(
        (picks[0] + picks[1]).astype(jnp.bfloat16),
        mask(iota(square, 0) < iota(square, 1), jnp.bfloat16),
        preferred_element_type=jnp.float32,
    )
    spots = iota((slots, local_tokens), 0)
    chosen = jnp.zeros((slots, local_tokens), jnp.float32)
    shares = jnp.zeros((slots, local_tokens), jnp.float32)
    for k in range(2):
        rank = jnp.sum(before * picks[k], axis=0, keepdims=True).astype(jnp.int32)
        found = spots == idr_ref[k : k + 1, :] * CAP + rank
        chosen = chosen + mask(found, jnp.float32)
        shares = shares + jnp.where(found, gv_ref[k : k + 1, :], 0.0)
    mixing[...] = shares
    picked = jnp.dot(
        chosen.astype(jnp.bfloat16), tok_ref[...], preferred_element_type=jnp.float32
    )
    packed[...] = picked.reshape(packed.shape).astype(jnp.bfloat16)

    loads[0].wait()
    loads[1].wait()
    for piece in range(FIRST):
        fill(w_send, piece, 1 - side)
    pl.semaphore_wait(barrier, 34)
    my_block = core * 2 + high

    def block_of(turn):
        return core * 2 + (high + turn) % 2

    def send_piece(piece):
        send(w_send.at[piece], w_all.at[piece, width:, :], w_sems, (piece,), mate)

    def wait_bytes(ref, sem):
        pltpu.make_async_copy(ref, ref, sem).wait()

    for turn in range(2):
        for other in (4, 3, 5, 2, 6, 1, 7, 0):
            to_high = (high + turn) % 2
            to_y = (y + other) % 8
            src = packed.at[to_high * 4 + to_y // 2]
            dst = x_near.at[my_block, :, y]
            if turn == 0 and other == 0:
                pltpu.make_async_copy(src, dst, route_sems.at[1, 0]).start()
            else:
                target = {"expert": to_high * 16 + to_y * 2 + core}
                remote(src, dst, route_sems, (turn,), target).start()
    for piece in range(FIRST):
        send_piece(piece)
    for piece in range(FIRST, PIECES):
        fill(w_send, piece, 1 - side)
    for piece in range(PIECES):
        fill(w_all, piece, side)
    for turn in range(2):
        block = block_of(turn)
        wait_bytes(x_near.at[block], route_sems.at[1, turn])
        send(x_near.at[block], x_far.at[block], mate_sems, (turn,), mate)
        send(x_near.at[block], x_near.at[block], near_sems, (turn,), sibling)
    for piece in range(FIRST, PIECES):
        send_piece(piece)
    loads[2].wait()
    fill_down(d_send, 1 - side)
    send(d_send, d_far, w_sems, (PIECES,), mate)
    for turn in range(2):
        block = block_of(turn)
        remote(x_near.at[block], x_far.at[block], mate_sems, (turn,), mate).wait_recv()
        send(x_far.at[block], x_far.at[block], far_sems, (turn,), sibling)
    fill_down(d_own, side)
    for turn in range(2):
        block = (1 - core) * 2 + (high + turn) % 2
        remote(x_near.at[block], x_near.at[block], near_sems, (turn,), sibling).wait_recv()
        remote(x_far.at[block], x_far.at[block], far_sems, (turn,), sibling).wait_recv()
    part_rows = rows // 4
    for block in range(4):
        for index, source in enumerate((x_near, x_far)):
            values = source[block].astype(jnp.float32).reshape(part_rows, width)
            x_all[
                block * part_rows : (block + 1) * part_rows, index * width : (index + 1) * width
            ] = values.astype(jnp.bfloat16)

    def rows_of(index):
        return pl.ds(pl.multiple_of(index * chunk, chunk), chunk)

    def wait_sum(way, hop, piece):
        remote(
            sum_out.at[way, hop - 1, piece],
            sum_in.at[way, hop - 1, piece],
            sum_sems,
            (way, hop - 1, piece),
            step[way],
        ).wait_recv()

    def wait_hidden(way, hop, part):
        origin = (z + ring - hop) % ring if way == 0 else (z + hop) % ring
        remote(
            hidden.at[origin, part],
            hidden.at[origin, part],
            gather_sems,
            (way, hop - 1, part),
            step[way],
        ).wait_recv()

    arrived = set()

    def ready(way, hop, part):
        if (way, hop, part) not in arrived:
            arrived.add((way, hop, part))
            wait_hidden(way, hop, part)

    def origin_of(slot):
        if slot % 2 == 1:
            return (z + ring - (slot + 1) // 2) % ring
        return (z + slot // 2) % ring

    row_tile = rows // 3
    part_units = units // PARTS
    per_part = PIECES // PARTS
    for kind, index, hop, way in schedule(half):
        if kind == "mul":
            remote(
                w_send.at[index], w_all.at[index, width:, :], w_sems, (index,), mate
            ).wait_recv()
            for tile in range(3):
                low = tile * row_tile
                parts[index, low : low + row_tile, :] = jnp.dot(
                    x_all[low : low + row_tile, :],
                    w_all[index],
                    preferred_element_type=jnp.float32,
                )
        elif kind == "sum":
            owner = (z + hop) % ring if way == 0 else (z + ring - hop) % ring
            total = parts[index, rows_of(owner), :]
            if runs(way, index, hop + 1, half):
                wait_sum(way, hop + 1, index)
                total = total + sum_in[way, hop, index].astype(jnp.float32)
            sum_out[way, hop - 1, index] = total.astype(jnp.bfloat16)
            send(
                sum_out.at[way, hop - 1, index],
                sum_in.at[way, hop - 1, index],
                sum_sems,
                (way, hop - 1, index),
                step[way],
            )
        elif kind == "act":
            total = parts[index, rows_of(z), :]
            for side_way in range(2):
                wait_sum(side_way, 1, index)
                total = total + sum_in[side_way, 0, index].astype(jnp.float32)
            gate = total[:, :cols]
            act = gate / (1.0 + jnp.exp(-gate)) * total[:, cols:]
            low = (index % per_part) * cols
            hidden[z, index // per_part, :, low : low + cols] = act.astype(jnp.bfloat16)
        elif kind == "gather":
            if hop > 1:
                ready(way, hop - 1, index)
            origin = (z + ring - hop + 1) % ring if way == 0 else (z + hop - 1) % ring
            send(
                hidden.at[origin, index],
                hidden.at[origin, index],
                gather_sems,
                (way, hop - 1, index),
                step[way],
            )
        elif kind == "down":
            if index == 0:
                remote(d_send, d_far, w_sems, (PIECES,), mate).wait_recv()
            for _, part, source_hop, source_way in sources_of(index, half):
                ready(source_way, source_hop, part)
            origin = origin_of(index)
            own = jnp.zeros((chunk, width), jnp.float32)
            far = jnp.zeros((chunk, width), jnp.float32)
            for part in range(PARTS):
                low = part * part_units
                lhs = hidden[origin, part]
                far = far + jnp.dot(
                    lhs, d_far[low : low + part_units, :], preferred_element_type=jnp.float32
                )
                own = own + jnp.dot(
                    lhs, d_own[low : low + part_units, :], preferred_element_type=jnp.float32
                )
            y_own[index] = own
            y_out[index] = far.astype(jnp.bfloat16)
            send(y_out.at[index], y_in.at[index], y_sems, (index,), mate)
        else:
            remote(y_out.at[index], y_in.at[index], y_sems, (index,), mate).wait_recv()
            total = y_own[index] + y_in[index].astype(jnp.float32)
            y_back[index * 8 : index * 8 + 8] = total.reshape(8, 8, width).astype(jnp.bfloat16)
            origin = origin_of(index)
            block = origin // 3
            dst = landed.at[share, expert, origin % 3]
            for other in range(8):
                to_y = (y + other) % 8
                src = y_back.at[index * 8 + to_y]
                target = {"expert": (block % 2) * 16 + to_y * 2 + block // 2}
                copy = remote(src, dst, back_sems, (), target)
                if other > 0:
                    copy.start()
                else:
                    pl.when(block != my_block)(copy.start)
                    pl.when(block == my_block)(
                        pltpu.make_async_copy(src, dst, back_sems.at[1]).start
                    )

    wait_bytes(landed, back_sems.at[1])
    sums = landed[0].astype(jnp.float32)
    for index in range(1, 4):
        sums = sums + landed[index].astype(jnp.float32)
    out_ref[...] = lax.dot_general(
        mixing[...],
        sums.reshape(slots, width),
        (((0,), (0,)), ((), ())),
        precision=lax.Precision.HIGHEST,
        preferred_element_type=jnp.float32,
    )

    wait_bytes(packed.at[:7], route_sems.at[0, 0])
    wait_bytes(packed, route_sems.at[0, 1])
    wait_bytes(y_back.at[:93], back_sems.at[0])
    for copy in sends:
        copy.wait_send()


def shards(tokens, expert_ids, gate_values, w_gate, w_up, w_down, scale_gate, scale_up, scale_down):
    ring = lax.axis_size("fsdp") // 2
    local_tokens, width = tokens.shape
    rows = lax.axis_size("expert") * CAP
    units = w_gate.shape[1] // 2
    cols = units // PIECES
    half = ring // 2
    chunk = rows // ring
    vmem = pl.BlockSpec(memory_space=pltpu.VMEM)
    smem = pl.BlockSpec(memory_space=pltpu.SMEM)
    bf16, f32 = jnp.bfloat16, jnp.float32
    dma = pltpu.SemaphoreType.DMA
    anywhere = pl.BlockSpec(memory_space=pl.ANY)
    mixed = pl.pallas_call(
        functools.partial(expert_kernel, ring),
        out_shape=jax.ShapeDtypeStruct((local_tokens, width), f32),
        in_specs=[vmem] * 3 + [anywhere] * 3 + [smem] * 3,
        out_specs=vmem,
        scratch_shapes=[
            pltpu.VMEM(w_gate.shape, bf16),
            pltpu.VMEM(w_up.shape, bf16),
            pltpu.VMEM(w_down.shape, bf16),
            pltpu.VMEM((EXPERTS, 3, 8, width), bf16),
            pltpu.VMEM((EXPERTS * CAP, local_tokens), f32),
            pltpu.VMEM((4, 3, 8, 8, width), bf16),
            pltpu.VMEM((4, 3, 8, 8, width), bf16),
            pltpu.VMEM((rows, 2 * width), bf16),
            pltpu.VMEM((PIECES, width, 2 * cols), bf16),
            pltpu.VMEM((PIECES, 2 * width, 2 * cols), bf16),
            pltpu.VMEM((units, width), bf16),
            pltpu.VMEM((units, width), bf16),
            pltpu.VMEM((units, width), bf16),
            pltpu.VMEM((PIECES, rows, 2 * cols), f32),
            pltpu.VMEM((2, half, PIECES, chunk, 2 * cols), bf16),
            pltpu.VMEM((2, half, PIECES, chunk, 2 * cols), bf16),
            pltpu.VMEM((ring, PARTS, chunk, units // PARTS), bf16),
            pltpu.VMEM((ring, chunk, width), f32),
            pltpu.VMEM((ring, chunk, width), bf16),
            pltpu.VMEM((ring, chunk, width), bf16),
            pltpu.VMEM((ring * 8, 8, width), bf16),
            pltpu.VMEM((4, EXPERTS, 3, 8, width), bf16),
            dma((2, 2)),
            dma((2, 2)),
            dma((2, 2)),
            dma((2, 2)),
            dma((2, PIECES + 1)),
            dma((2, 2, half, PIECES)),
            dma((2, 2, half, PARTS)),
            dma((2, ring)),
            dma((2,)),
            dma((3,)),
        ],
        compiler_params=pltpu.CompilerParams(collective_id=0, has_side_effects=True),
        name="expert_layer",
    )(
        expert_ids.T,
        gate_values.T,
        tokens,
        w_gate,
        w_up,
        w_down,
        scale_gate,
        scale_up,
        scale_down.T,
    )
    return mixed.astype(bf16)


def solution(mesh):
    in_specs = (
        P("expert", "fsdp"),
        P("expert", None),
        P("expert", None),
        P("fsdp", "expert"),
        P("fsdp", "expert"),
        P("expert", "fsdp"),
        P("fsdp", "expert"),
        P("fsdp", "expert"),
        P("expert", "fsdp"),
    )
    out_specs = P("expert", "fsdp")
    return jax.shard_map(shards, mesh=mesh, in_specs=in_specs, out_specs=out_specs, check_vma=False)
```

```python
import functools

import jax
import jax.numpy as jnp
from jax import lax
from jax.experimental import pallas as pl
from jax.experimental.pallas import tpu as pltpu
from jax.sharding import PartitionSpec as P

EXPERTS = 8
BLOCK = 128
CAP = 24
PIECES = 8
PARTS = 4
FIRST = 3
X_AT = 21.0
W_AT = (7.5, 10.6, 13.7, 21.5, 24.6, 27.7, 30.8, 33.9)
D_AT = 46.6
COPY_LAG = 2.0
CHUNK_TIME = 6.24
MESH = pl.DeviceIdType.MESH


def runs(way, piece, hop, half):
    return 1 <= hop < half or (hop == half and piece // (PIECES // 2) == way)


def gathers(way, part, hop, half):
    return 1 <= hop < half or (hop == half and part // (PARTS // 2) == way)


def sources_of(slot, half):
    if slot == 0:
        return []
    if slot == 2 * half - 1:
        return [("gather", part, half, part // (PARTS // 2)) for part in range(PARTS)]
    hop, way = (slot + 1) // 2, (slot + 1) % 2
    return [("gather", part, hop, way) for part in range(PARTS)]


def schedule(half):
    ways, hops = (0, 1), range(1, half + 1)
    cost = dict(mul=0.45, sum=0.12, act=0.2, gather=0.05, down=0.28, back=0.35)
    rank = dict(gather=1, act=1, sum=1, mul=2, back=3, down=4)
    left = [("mul", piece, 0, 0) for piece in range(PIECES)]
    left += [
        ("sum", piece, hop, way)
        for piece in range(PIECES)
        for hop in hops
        for way in ways
        if runs(way, piece, hop, half)
    ]
    left += [("act", piece, 0, 0) for piece in range(PIECES)]
    left += [
        ("gather", part, hop, way)
        for part in range(PARTS)
        for hop in hops
        for way in ways
        if gathers(way, part, hop, half)
    ]
    left += [("down", slot, part, 0) for slot in range(2 * half) for part in range(PARTS)]
    left += [("back", slot, 0, 0) for slot in range(2 * half)]
    done, landing, joined = {}, {}, {}

    def ready(task):
        kind, index, hop, way = task
        per = PIECES // PARTS
        if kind == "mul":
            return max(X_AT, W_AT[index])
        if kind == "sum":
            needs = [done.get(("mul", index, 0, 0))]
            if runs(way, index, hop + 1, half):
                needs.append(landing.get(("sum", index, hop + 1, way)))
        elif kind == "act":
            needs = [landing.get(("sum", index, 1, side)) for side in ways]
        elif kind == "gather" and hop == 1:
            needs = [done.get(("act", index * per + k, 0, 0)) for k in range(per)]
        elif kind == "gather":
            needs = [landing.get(("gather", index, hop - 1, way))]
        elif kind == "down" and index == 0:
            needs = [D_AT] + [done.get(("act", hop * per + k, 0, 0)) for k in range(per)]
        elif kind == "down":
            needs = [D_AT, landing.get(sources_of(index, half)[hop])]
        else:
            needs = [landing.get(("down", index))]
        return None if None in needs else max(needs)

    now, links, order = 0.0, {0: 0.0, 1: 0.0, "mate": D_AT}, []
    while left:
        waiting = [(ready(task), task) for task in left]
        waiting = [entry for entry in waiting if entry[0] is not None]
        now = max(now, min(entry[0] for entry in waiting))
        able = [entry for entry in waiting if entry[0] <= now]
        _, task = min(able, key=lambda entry: (rank[entry[1][0]], entry[0], entry[1]))
        left.remove(task)
        order.append(task)
        kind, _, _, way = task
        now += cost[kind]
        done[task] = now
        if kind == "sum" or kind == "gather":
            load = CHUNK_TIME / PIECES if kind == "sum" else CHUNK_TIME / 2 / PARTS
            links[way] = max(links[way], now) + load
            landing[task] = links[way] + COPY_LAG
        elif kind == "down":
            slot = task[1]
            joined[slot] = joined.get(slot, 0) + 1
            if joined[slot] == PARTS:
                links["mate"] = max(links["mate"], now) + CHUNK_TIME / 8
                landing[("down", slot)] = links["mate"] + COPY_LAG
    return order


def expert_kernel(
    ring,
    idr_ref,
    gv_ref,
    tok_ref,
    wg_any,
    wu_any,
    wd_any,
    sg_ref,
    su_ref,
    sd_ref,
    out_ref,
    wg_ref,
    wu_ref,
    wd_ref,
    packed,
    mixing,
    x_near,
    x_far,
    x_all,
    w_send,
    w_all,
    d_send,
    d_own,
    d_far,
    parts,
    sum_out,
    sum_in,
    hidden,
    y_own,
    y_far,
    y_out,
    y_in,
    y_back,
    landed,
    route_sems,
    mate_sems,
    near_sems,
    far_sems,
    w_sems,
    sum_sems,
    gather_sems,
    y_sems,
    back_sems,
    load_sems,
    spread,
):
    half = ring // 2
    local_tokens, width = tok_ref.shape
    rows = x_all.shape[0]
    chunk = rows // ring
    units = wg_ref.shape[1] // 2
    cols = units // PIECES
    slots = EXPERTS * CAP
    place = lax.axis_index("fsdp")
    z = place // 2
    side = place % 2
    seat = lax.axis_index("expert")
    high = seat // 16
    y = (seat // 2) % 8
    core = seat % 2
    expert = high * 4 + y // 2
    share = (y % 2) * 2 + core
    mate = {"fsdp": z * 2 + (1 - side)}
    sibling = {"expert": seat + 1 - 2 * core}
    step = {
        0: {"fsdp": ((z + 1) % ring) * 2 + side},
        1: {"fsdp": ((z + ring - 1) % ring) * 2 + side},
    }
    sends = []

    def remote(src, dst, sems, index, target):
        return pltpu.make_async_remote_copy(
            src_ref=src,
            dst_ref=dst,
            send_sem=sems.at[(0,) + index],
            recv_sem=sems.at[(1,) + index],
            device_id=target,
            device_id_type=MESH,
        )

    def send(*args):
        copy = remote(*args)
        copy.start()
        sends.append(copy)

    loads = [
        pltpu.make_async_copy(src, dst, load_sems.at[index])
        for index, (src, dst) in enumerate(((wg_any, wg_ref), (wu_any, wu_ref), (wd_any, wd_ref)))
    ]
    for load in loads:
        load.start()
    barrier = pltpu.get_barrier_semaphore()

    def along(count):
        return {"expert": high * 16 + (y + 8 + count) % 8 * 2 + core}

    across = {"expert": (seat + 16) % 32}

    def tell(sem, targets):
        for target in targets:
            pl.semaphore_signal(sem, inc=1, device_id=target, device_id_type=MESH)

    tell(barrier, (mate, step[0], step[1], sibling, along(1), along(-1), across))

    def scaled(w_ref, s_ref, block, start):
        tiles = []
        for lane in range(cols // BLOCK):
            low = pl.multiple_of(start + lane * BLOCK, BLOCK)
            values = w_ref[block * BLOCK : (block + 1) * BLOCK, pl.ds(low, BLOCK)]
            scale = s_ref[block, start // BLOCK + lane]
            tiles.append((values.astype(jnp.float32) * scale).astype(jnp.bfloat16))
        return tiles

    def fill(dst, piece, owner):
        for block in range(width // BLOCK):
            low = block * BLOCK
            start = owner * units + piece * cols
            for index, (w_ref, s_ref) in enumerate(((wg_ref, sg_ref), (wu_ref, su_ref))):
                for lane, tile in enumerate(scaled(w_ref, s_ref, block, start)):
                    left = index * cols + lane * BLOCK
                    dst[piece, low : low + BLOCK, left : left + BLOCK] = tile

    def fill_down(dst, owner):
        for block in range(units // BLOCK):
            start = pl.multiple_of(owner * units + block * BLOCK, BLOCK)
            for lane in range(width // BLOCK):
                left = lane * BLOCK
                scale = sd_ref[lane, owner * (units // BLOCK) + block]
                values = wd_ref[pl.ds(start, BLOCK), left : left + BLOCK].astype(jnp.float32)
                dst[block * BLOCK : (block + 1) * BLOCK, left : left + BLOCK] = (
                    values * scale
                ).astype(jnp.bfloat16)

    def iota(shape, axis):
        return lax.broadcasted_iota(jnp.int32, shape, axis)

    def mask(test, kind):
        return jnp.where(test, 1.0, 0.0).astype(kind)

    loads[0].wait()
    loads[1].wait()
    for piece in range(FIRST):
        fill(w_send, piece, 1 - side)
    pl.semaphore_wait(barrier, 7)
    my_block = core * 2 + high

    def block_of(turn):
        return core * 2 + (high + turn) % 2

    def send_piece(piece):
        send(w_send.at[piece], w_all.at[piece, width:, :], w_sems, (piece,), mate)

    def wait_bytes(ref, sem):
        pltpu.make_async_copy(ref, ref, sem).wait()

    for piece in range(FIRST):
        send_piece(piece)
    tell(spread.at[0], (along(1), along(-1)))
    square = (local_tokens, local_tokens)
    names = iota((EXPERTS, local_tokens), 0)
    picks = [mask(names == idr_ref[k : k + 1, :], jnp.float32) for k in range(2)]
    before = jnp.dot(
        (picks[0] + picks[1]).astype(jnp.bfloat16),
        mask(iota(square, 0) < iota(square, 1), jnp.bfloat16),
        preferred_element_type=jnp.float32,
    )
    spots = iota((slots, local_tokens), 0)
    chosen = jnp.zeros((slots, local_tokens), jnp.float32)
    shares = jnp.zeros((slots, local_tokens), jnp.float32)
    for k in range(2):
        rank = jnp.sum(before * picks[k], axis=0, keepdims=True).astype(jnp.int32)
        found = spots == idr_ref[k : k + 1, :] * CAP + rank
        chosen = chosen + mask(found, jnp.float32)
        shares = shares + jnp.where(found, gv_ref[k : k + 1, :], 0.0)
    mixing[...] = shares
    picked = jnp.dot(
        chosen.astype(jnp.bfloat16), tok_ref[...], preferred_element_type=jnp.float32
    )
    packed[...] = picked.reshape(packed.shape).astype(jnp.bfloat16)

    pl.semaphore_wait(spread.at[0], 2)
    tell(spread.at[1], (along(2), along(-2)))
    fill(w_send, FIRST, 1 - side)
    pl.semaphore_wait(spread.at[1], 2)
    tell(spread.at[2], (across,))
    fill(w_send, FIRST + 1, 1 - side)
    pl.semaphore_wait(spread.at[2], 1)
    tell(spread.at[3], (sibling,))
    for turn in range(2):
        for other in (4, 3, 5, 2, 6, 1, 7, 0):
            to_high = (high + turn) % 2
            to_y = (y + other) % 8
            src = packed.at[to_high * 4 + to_y // 2]
            dst = x_near.at[my_block, :, y]
            if turn == 0 and other == 0:
                pltpu.make_async_copy(src, dst, route_sems.at[1, 0]).start()
            else:
                target = {"expert": to_high * 16 + to_y * 2 + core}
                remote(src, dst, route_sems, (turn,), target).start()
    for piece in range(FIRST + 2, PIECES):
        fill(w_send, piece, 1 - side)
    for piece in range(PIECES):
        fill(w_all, piece, side)
    for turn in range(2):
        block = block_of(turn)
        wait_bytes(x_near.at[block], route_sems.at[1, turn])
        send(x_near.at[block], x_far.at[block], mate_sems, (turn,), mate)
        send(x_near.at[block], x_near.at[block], near_sems, (turn,), sibling)
    for piece in range(FIRST, PIECES):
        send_piece(piece)
    loads[2].wait()
    fill_down(d_send, 1 - side)
    send(d_send, d_far, w_sems, (PIECES,), mate)
    for turn in range(2):
        block = block_of(turn)
        remote(x_near.at[block], x_far.at[block], mate_sems, (turn,), mate).wait_recv()
        send(x_far.at[block], x_far.at[block], far_sems, (turn,), sibling)
    fill_down(d_own, side)
    for turn in range(2):
        block = (1 - core) * 2 + (high + turn) % 2
        remote(x_near.at[block], x_near.at[block], near_sems, (turn,), sibling).wait_recv()
        remote(x_far.at[block], x_far.at[block], far_sems, (turn,), sibling).wait_recv()
    part_rows = rows // 4
    for block in range(4):
        for index, source in enumerate((x_near, x_far)):
            values = source[block].astype(jnp.float32).reshape(part_rows, width)
            x_all[
                block * part_rows : (block + 1) * part_rows, index * width : (index + 1) * width
            ] = values.astype(jnp.bfloat16)

    def rows_of(index):
        return pl.ds(pl.multiple_of(index * chunk, chunk), chunk)

    def wait_sum(way, hop, piece):
        remote(
            sum_out.at[way, hop - 1, piece],
            sum_in.at[way, hop - 1, piece],
            sum_sems,
            (way, hop - 1, piece),
            step[way],
        ).wait_recv()

    def wait_hidden(way, hop, part):
        origin = (z + ring - hop) % ring if way == 0 else (z + hop) % ring
        remote(
            hidden.at[origin, part],
            hidden.at[origin, part],
            gather_sems,
            (way, hop - 1, part),
            step[way],
        ).wait_recv()

    arrived = set()

    def ready(way, hop, part):
        if (way, hop, part) not in arrived:
            arrived.add((way, hop, part))
            wait_hidden(way, hop, part)

    def origin_of(slot):
        if slot % 2 == 1:
            return (z + ring - (slot + 1) // 2) % ring
        return (z + slot // 2) % ring

    row_tile = rows // 3
    part_units = units // PARTS
    per_part = PIECES // PARTS
    joined = {}
    told = False
    for kind, index, hop, way in schedule(half):
        if kind == "mul":
            remote(
                w_send.at[index], w_all.at[index, width:, :], w_sems, (index,), mate
            ).wait_recv()
            for tile in range(3):
                low = tile * row_tile
                parts[index, low : low + row_tile, :] = jnp.dot(
                    x_all[low : low + row_tile, :],
                    w_all[index],
                    preferred_element_type=jnp.float32,
                )
        elif kind == "sum":
            owner = (z + hop) % ring if way == 0 else (z + ring - hop) % ring
            total = parts[index, rows_of(owner), :]
            if runs(way, index, hop + 1, half):
                wait_sum(way, hop + 1, index)
                total = total + sum_in[way, hop, index].astype(jnp.float32)
            sum_out[way, hop - 1, index] = total.astype(jnp.bfloat16)
            send(
                sum_out.at[way, hop - 1, index],
                sum_in.at[way, hop - 1, index],
                sum_sems,
                (way, hop - 1, index),
                step[way],
            )
        elif kind == "act":
            total = parts[index, rows_of(z), :]
            for side_way in range(2):
                wait_sum(side_way, 1, index)
                total = total + sum_in[side_way, 0, index].astype(jnp.float32)
            gate = total[:, :cols]
            act = gate / (1.0 + jnp.exp(-gate)) * total[:, cols:]
            low = (index % per_part) * cols
            hidden[z, index // per_part, :, low : low + cols] = act.astype(jnp.bfloat16)
        elif kind == "gather":
            if hop > 1:
                ready(way, hop - 1, index)
            origin = (z + ring - hop + 1) % ring if way == 0 else (z + hop - 1) % ring
            send(
                hidden.at[origin, index],
                hidden.at[origin, index],
                gather_sems,
                (way, hop - 1, index),
                step[way],
            )
        elif kind == "down":
            if not joined:
                remote(d_send, d_far, w_sems, (PIECES,), mate).wait_recv()
            if index > 0:
                _, _, source_hop, source_way = sources_of(index, half)[hop]
                ready(source_way, source_hop, hop)
            lhs = hidden[origin_of(index), hop]
            low = hop * part_units
            far = jnp.dot(
                lhs, d_far[low : low + part_units, :], preferred_element_type=jnp.float32
            )
            own = jnp.dot(
                lhs, d_own[low : low + part_units, :], preferred_element_type=jnp.float32
            )
            count = joined[index] = joined.get(index, 0) + 1
            if count > 1:
                far = far + y_far[index]
                own = own + y_own[index]
            y_own[index] = own
            if count < PARTS:
                y_far[index] = far
            else:
                y_out[index] = far.astype(jnp.bfloat16)
                send(y_out.at[index], y_in.at[index], y_sems, (index,), mate)
        else:
            if not told:
                pl.semaphore_wait(spread.at[3], 1)
                told = True
            remote(y_out.at[index], y_in.at[index], y_sems, (index,), mate).wait_recv()
            total = y_own[index] + y_in[index].astype(jnp.float32)
            y_back[index * 8 : index * 8 + 8] = total.reshape(8, 8, width).astype(jnp.bfloat16)
            origin = origin_of(index)
            block = origin // 3
            dst = landed.at[share, expert, origin % 3]
            for other in (4, 3, 5, 2, 6, 1, 7, 0):
                to_y = (y + other) % 8
                src = y_back.at[index * 8 + to_y]
                target = {"expert": (block % 2) * 16 + to_y * 2 + block // 2}
                copy = remote(src, dst, back_sems, (), target)
                if other > 0:
                    copy.start()
                else:
                    pl.when(block != my_block)(copy.start)
                    pl.when(block == my_block)(
                        pltpu.make_async_copy(src, dst, back_sems.at[1]).start
                    )

    wait_bytes(landed, back_sems.at[1])
    sums = landed[0].astype(jnp.float32)
    for index in range(1, 4):
        sums = sums + landed[index].astype(jnp.float32)
    out_ref[...] = lax.dot_general(
        mixing[...],
        sums.reshape(slots, width),
        (((0,), (0,)), ((), ())),
        precision=lax.Precision.HIGHEST,
        preferred_element_type=jnp.float32,
    )

    wait_bytes(packed.at[:7], route_sems.at[0, 0])
    wait_bytes(packed, route_sems.at[0, 1])
    wait_bytes(y_back.at[:93], back_sems.at[0])
    for copy in sends:
        copy.wait_send()


def shards(tokens, expert_ids, gate_values, w_gate, w_up, w_down, scale_gate, scale_up, scale_down):
    ring = lax.axis_size("fsdp") // 2
    local_tokens, width = tokens.shape
    rows = lax.axis_size("expert") * CAP
    units = w_gate.shape[1] // 2
    cols = units // PIECES
    half = ring // 2
    chunk = rows // ring
    vmem = pl.BlockSpec(memory_space=pltpu.VMEM)
    smem = pl.BlockSpec(memory_space=pltpu.SMEM)
    bf16, f32 = jnp.bfloat16, jnp.float32
    dma = pltpu.SemaphoreType.DMA
    anywhere = pl.BlockSpec(memory_space=pl.ANY)
    mixed = pl.pallas_call(
        functools.partial(expert_kernel, ring),
        out_shape=jax.ShapeDtypeStruct((local_tokens, width), f32),
        in_specs=[vmem] * 3 + [anywhere] * 3 + [smem] * 3,
        out_specs=vmem,
        scratch_shapes=[
            pltpu.VMEM(w_gate.shape, bf16),
            pltpu.VMEM(w_up.shape, bf16),
            pltpu.VMEM(w_down.shape, bf16),
            pltpu.VMEM((EXPERTS, 3, 8, width), bf16),
            pltpu.VMEM((EXPERTS * CAP, local_tokens), f32),
            pltpu.VMEM((4, 3, 8, 8, width), bf16),
            pltpu.VMEM((4, 3, 8, 8, width), bf16),
            pltpu.VMEM((rows, 2 * width), bf16),
            pltpu.VMEM((PIECES, width, 2 * cols), bf16),
            pltpu.VMEM((PIECES, 2 * width, 2 * cols), bf16),
            pltpu.VMEM((units, width), bf16),
            pltpu.VMEM((units, width), bf16),
            pltpu.VMEM((units, width), bf16),
            pltpu.VMEM((PIECES, rows, 2 * cols), f32),
            pltpu.VMEM((2, half, PIECES, chunk, 2 * cols), bf16),
            pltpu.VMEM((2, half, PIECES, chunk, 2 * cols), bf16),
            pltpu.VMEM((ring, PARTS, chunk, units // PARTS), bf16),
            pltpu.VMEM((ring, chunk, width), f32),
            pltpu.VMEM((ring, chunk, width), f32),
            pltpu.VMEM((ring, chunk, width), bf16),
            pltpu.VMEM((ring, chunk, width), bf16),
            pltpu.VMEM((ring * 8, 8, width), bf16),
            pltpu.VMEM((4, EXPERTS, 3, 8, width), bf16),
            dma((2, 2)),
            dma((2, 2)),
            dma((2, 2)),
            dma((2, 2)),
            dma((2, PIECES + 1)),
            dma((2, 2, half, PIECES)),
            dma((2, 2, half, PARTS)),
            dma((2, ring)),
            dma((2,)),
            dma((3,)),
            pltpu.SemaphoreType.REGULAR((4,)),
        ],
        compiler_params=pltpu.CompilerParams(collective_id=0, has_side_effects=True),
        name="expert_layer",
    )(
        expert_ids.T,
        gate_values.T,
        tokens,
        w_gate,
        w_up,
        w_down,
        scale_gate,
        scale_up,
        scale_down.T,
    )
    return mixed.astype(bf16)


def solution(mesh):
    in_specs = (
        P("expert", "fsdp"),
        P("expert", None),
        P("expert", None),
        P("fsdp", "expert"),
        P("fsdp", "expert"),
        P("expert", "fsdp"),
        P("fsdp", "expert"),
        P("fsdp", "expert"),
        P("expert", "fsdp"),
    )
    out_specs = P("expert", "fsdp")
    return jax.shard_map(shards, mesh=mesh, in_specs=in_specs, out_specs=out_specs, check_vma=False)
```

```python
import functools

import jax
import jax.numpy as jnp
from jax import lax
from jax.experimental import pallas as pl
from jax.experimental.pallas import tpu as pltpu
from jax.sharding import PartitionSpec as P

EXPERTS = 8
BLOCK = 128
CAP = 24
PIECES = 8
PARTS = 4
FIRST = 3
X_AT = 21.0
W_AT = (7.5, 10.6, 13.7, 21.5, 24.6, 27.7, 30.8, 33.9)
D_AT = 46.6
COPY_LAG = 2.0
CHUNK_TIME = 6.24
MESH = pl.DeviceIdType.MESH


def runs(way, piece, hop, half):
    return 1 <= hop < half or (hop == half and piece // (PIECES // 2) == way)


def gathers(way, part, hop, half):
    return 1 <= hop < half or (hop == half and part // (PARTS // 2) == way)


def sources_of(slot, half):
    if slot == 0:
        return []
    if slot == 2 * half - 1:
        return [("gather", part, half, part // (PARTS // 2)) for part in range(PARTS)]
    hop, way = (slot + 1) // 2, (slot + 1) % 2
    return [("gather", part, hop, way) for part in range(PARTS)]


def schedule(half):
    ways, hops = (0, 1), range(1, half + 1)
    cost = dict(mul=0.45, sum=0.12, act=0.2, gather=0.05, down=0.28, back=0.35)
    rank = dict(gather=1, act=1, sum=1, mul=2, back=3, down=4)
    left = [("mul", piece, 0, 0) for piece in range(PIECES)]
    left += [
        ("sum", piece, hop, way)
        for piece in range(PIECES)
        for hop in hops
        for way in ways
        if runs(way, piece, hop, half)
    ]
    sums = left[PIECES:]
    left += [("act", piece, 0, 0) for piece in range(PIECES)]
    left += [
        ("gather", part, hop, way)
        for part in range(PARTS)
        for hop in hops
        for way in ways
        if gathers(way, part, hop, half)
    ]
    left += [("down", slot, part, 0) for slot in range(2 * half) for part in range(PARTS)]
    left += [("back", slot, 0, 0) for slot in range(2 * half)]
    done, landing, joined = {}, {}, {}

    def ready(task):
        kind, index, hop, way = task
        per = PIECES // PARTS
        if kind == "mul":
            return max(X_AT, W_AT[index])
        if kind == "sum":
            needs = [done.get(("mul", index, 0, 0))]
            if runs(way, index, hop + 1, half):
                needs.append(landing.get(("sum", index, hop + 1, way)))
        elif kind == "act":
            needs = [landing.get(("sum", index, 1, side)) for side in ways]
        elif kind == "gather" and hop == 1:
            needs = [done.get(("act", index * per + k, 0, 0)) for k in range(per)]
            needs += [done.get(other) for other in sums]
        elif kind == "gather":
            needs = [landing.get(("gather", index, hop - 1, way))]
        elif kind == "down" and index == 0:
            needs = [D_AT] + [done.get(("act", hop * per + k, 0, 0)) for k in range(per)]
        elif kind == "down":
            needs = [D_AT, landing.get(sources_of(index, half)[hop])]
        else:
            needs = [landing.get(("down", index))]
        return None if None in needs else max(needs)

    now, links, order = 0.0, {0: 0.0, 1: 0.0, "mate": D_AT}, []
    while left:
        waiting = [(ready(task), task) for task in left]
        waiting = [entry for entry in waiting if entry[0] is not None]
        now = max(now, min(entry[0] for entry in waiting))
        able = [entry for entry in waiting if entry[0] <= now]
        _, task = min(able, key=lambda entry: (rank[entry[1][0]], entry[0], entry[1]))
        left.remove(task)
        order.append(task)
        kind, _, _, way = task
        now += cost[kind]
        done[task] = now
        if kind == "sum" or kind == "gather":
            load = CHUNK_TIME / PIECES if kind == "sum" else CHUNK_TIME / 2 / PARTS
            links[way] = max(links[way], now) + load
            landing[task] = links[way] + COPY_LAG
        elif kind == "down":
            slot = task[1]
            joined[slot] = joined.get(slot, 0) + 1
            if joined[slot] == PARTS:
                links["mate"] = max(links["mate"], now) + CHUNK_TIME / 8
                landing[("down", slot)] = links["mate"] + COPY_LAG
    return order


def expert_kernel(
    ring,
    idr_ref,
    gv_ref,
    tok_ref,
    wg_any,
    wu_any,
    wd_any,
    sg_ref,
    su_ref,
    sd_ref,
    out_ref,
    wg_ref,
    wu_ref,
    wd_ref,
    packed,
    mixing,
    x_near,
    x_far,
    x_all,
    w_send,
    w_all,
    d_send,
    d_own,
    d_far,
    parts,
    sum_out,
    sum_in,
    hidden,
    y_own,
    y_far,
    y_out,
    y_in,
    y_back,
    landed,
    route_sems,
    mate_sems,
    near_sems,
    far_sems,
    w_sems,
    sum_sems,
    gather_sems,
    y_sems,
    back_sems,
    load_sems,
    spread,
):
    half = ring // 2
    local_tokens, width = tok_ref.shape
    rows = x_all.shape[0]
    chunk = rows // ring
    units = wg_ref.shape[1] // 2
    cols = units // PIECES
    slots = EXPERTS * CAP
    place = lax.axis_index("fsdp")
    z = place // 2
    side = place % 2
    seat = lax.axis_index("expert")
    high = seat // 16
    y = (seat // 2) % 8
    core = seat % 2
    expert = high * 4 + y // 2
    share = (y % 2) * 2 + core
    mate = {"fsdp": z * 2 + (1 - side)}
    sibling = {"expert": seat + 1 - 2 * core}
    step = {
        0: {"fsdp": ((z + 1) % ring) * 2 + side},
        1: {"fsdp": ((z + ring - 1) % ring) * 2 + side},
    }
    sends = []

    def remote(src, dst, sems, index, target):
        return pltpu.make_async_remote_copy(
            src_ref=src,
            dst_ref=dst,
            send_sem=sems.at[(0,) + index],
            recv_sem=sems.at[(1,) + index],
            device_id=target,
            device_id_type=MESH,
        )

    def send(*args):
        copy = remote(*args)
        copy.start()
        sends.append(copy)

    loads = [
        pltpu.make_async_copy(src, dst, load_sems.at[index])
        for index, (src, dst) in enumerate(((wg_any, wg_ref), (wu_any, wu_ref), (wd_any, wd_ref)))
    ]
    for load in loads:
        load.start()
    barrier = pltpu.get_barrier_semaphore()

    def along(count):
        return {"expert": high * 16 + (y + 8 + count) % 8 * 2 + core}

    across = {"expert": (seat + 16) % 32}

    def tell(sem, targets):
        for target in targets:
            pl.semaphore_signal(sem, inc=1, device_id=target, device_id_type=MESH)

    tell(barrier, (mate, step[0], step[1], sibling, along(1), along(-1), across))

    def scaled(w_ref, s_ref, block, start):
        tiles = []
        for lane in range(cols // BLOCK):
            low = pl.multiple_of(start + lane * BLOCK, BLOCK)
            values = w_ref[block * BLOCK : (block + 1) * BLOCK, pl.ds(low, BLOCK)]
            scale = s_ref[block, start // BLOCK + lane]
            tiles.append((values.astype(jnp.float32) * scale).astype(jnp.bfloat16))
        return tiles

    def fill(dst, piece, owner):
        for block in range(width // BLOCK):
            low = block * BLOCK
            start = owner * units + piece * cols
            for index, (w_ref, s_ref) in enumerate(((wg_ref, sg_ref), (wu_ref, su_ref))):
                for lane, tile in enumerate(scaled(w_ref, s_ref, block, start)):
                    left = index * cols + lane * BLOCK
                    dst[piece, low : low + BLOCK, left : left + BLOCK] = tile

    def fill_down(dst, owner):
        for block in range(units // BLOCK):
            start = pl.multiple_of(owner * units + block * BLOCK, BLOCK)
            for lane in range(width // BLOCK):
                left = lane * BLOCK
                scale = sd_ref[lane, owner * (units // BLOCK) + block]
                values = wd_ref[pl.ds(start, BLOCK), left : left + BLOCK].astype(jnp.float32)
                dst[block * BLOCK : (block + 1) * BLOCK, left : left + BLOCK] = (
                    values * scale
                ).astype(jnp.bfloat16)

    def iota(shape, axis):
        return lax.broadcasted_iota(jnp.int32, shape, axis)

    def mask(test, kind):
        return jnp.where(test, 1.0, 0.0).astype(kind)

    square = (local_tokens, local_tokens)
    names = iota((EXPERTS, local_tokens), 0)
    picks = [mask(names == idr_ref[k : k + 1, :], jnp.float32) for k in range(2)]
    before = jnp.dot(
        (picks[0] + picks[1]).astype(jnp.bfloat16),
        mask(iota(square, 0) < iota(square, 1), jnp.bfloat16),
        preferred_element_type=jnp.float32,
    )
    spots = iota((slots, local_tokens), 0)
    chosen = jnp.zeros((slots, local_tokens), jnp.float32)
    shares = jnp.zeros((slots, local_tokens), jnp.float32)
    for k in range(2):
        rank = jnp.sum(before * picks[k], axis=0, keepdims=True).astype(jnp.int32)
        found = spots == idr_ref[k : k + 1, :] * CAP + rank
        chosen = chosen + mask(found, jnp.float32)
        shares = shares + jnp.where(found, gv_ref[k : k + 1, :], 0.0)
    mixing[...] = shares
    picked = jnp.dot(
        chosen.astype(jnp.bfloat16), tok_ref[...], preferred_element_type=jnp.float32
    )
    packed[...] = picked.reshape(packed.shape).astype(jnp.bfloat16)

    loads[0].wait()
    loads[1].wait()
    fill(w_send, 0, 1 - side)
    pl.semaphore_wait(barrier, 7)
    my_block = core * 2 + high

    def block_of(turn):
        return core * 2 + (high + turn) % 2

    def send_piece(piece):
        send(w_send.at[piece], w_all.at[piece, width:, :], w_sems, (piece,), mate)

    def wait_bytes(ref, sem):
        pltpu.make_async_copy(ref, ref, sem).wait()

    tell(spread.at[0], (along(1), along(-1)))
    send_piece(0)
    fill(w_send, 1, 1 - side)
    send_piece(1)
    pl.semaphore_wait(spread.at[0], 2)
    tell(spread.at[1], (along(2), along(-2)))
    fill(w_send, 2, 1 - side)
    send_piece(2)
    pl.semaphore_wait(spread.at[1], 2)
    tell(spread.at[2], (across,))
    pl.semaphore_wait(spread.at[2], 1)
    for turn in range(2):
        for other in (4, 3, 5, 2, 6, 1, 7, 0):
            to_high = (high + turn) % 2
            to_y = (y + other) % 8
            src = packed.at[to_high * 4 + to_y // 2]
            dst = x_near.at[my_block, :, y]
            if turn == 0 and other == 0:
                pltpu.make_async_copy(src, dst, route_sems.at[1, 0]).start()
            else:
                target = {"expert": to_high * 16 + to_y * 2 + core}
                remote(src, dst, route_sems, (turn,), target).start()
    tell(spread.at[3], (sibling,))
    for piece in range(FIRST, PIECES):
        fill(w_send, piece, 1 - side)
    for piece in range(PIECES):
        fill(w_all, piece, side)
    for turn in range(2):
        block = block_of(turn)
        wait_bytes(x_near.at[block], route_sems.at[1, turn])
        send(x_near.at[block], x_far.at[block], mate_sems, (turn,), mate)
        send(x_near.at[block], x_near.at[block], near_sems, (turn,), sibling)
    for piece in range(FIRST, PIECES):
        send_piece(piece)
    loads[2].wait()
    fill_down(d_send, 1 - side)
    send(d_send, d_far, w_sems, (PIECES,), mate)
    part_rows = rows // 4

    def assemble(source, index, block):
        values = source[block].astype(jnp.float32).reshape(part_rows, width)
        span = pl.ds(pl.multiple_of(block * part_rows, part_rows), part_rows)
        x_all[span, index * width : (index + 1) * width] = values.astype(jnp.bfloat16)

    for turn in range(2):
        assemble(x_near, 0, block_of(turn))
    for turn in range(2):
        block = block_of(turn)
        remote(x_near.at[block], x_far.at[block], mate_sems, (turn,), mate).wait_recv()
        send(x_far.at[block], x_far.at[block], far_sems, (turn,), sibling)
    for turn in range(2):
        assemble(x_far, 1, block_of(turn))
    for turn in range(2):
        block = (1 - core) * 2 + (high + turn) % 2
        remote(x_near.at[block], x_near.at[block], near_sems, (turn,), sibling).wait_recv()
        assemble(x_near, 0, block)
        remote(x_far.at[block], x_far.at[block], far_sems, (turn,), sibling).wait_recv()
        assemble(x_far, 1, block)
    def rows_of(index):
        return pl.ds(pl.multiple_of(index * chunk, chunk), chunk)

    def wait_sum(way, hop, piece):
        remote(
            sum_out.at[way, hop - 1, piece],
            sum_in.at[way, hop - 1, piece],
            sum_sems,
            (way, hop - 1, piece),
            step[way],
        ).wait_recv()

    def wait_hidden(way, hop, part):
        origin = (z + ring - hop) % ring if way == 0 else (z + hop) % ring
        remote(
            hidden.at[origin, part],
            hidden.at[origin, part],
            gather_sems,
            (way, hop - 1, part),
            step[way],
        ).wait_recv()

    arrived = set()

    def ready(way, hop, part):
        if (way, hop, part) not in arrived:
            arrived.add((way, hop, part))
            wait_hidden(way, hop, part)

    def origin_of(slot):
        if slot % 2 == 1:
            return (z + ring - (slot + 1) // 2) % ring
        return (z + slot // 2) % ring

    row_tile = rows // 3
    part_units = units // PARTS
    per_part = PIECES // PARTS
    joined = {}
    told = False
    for kind, index, hop, way in schedule(half):
        if kind == "mul":
            remote(
                w_send.at[index], w_all.at[index, width:, :], w_sems, (index,), mate
            ).wait_recv()
            for tile in range(3):
                low = tile * row_tile
                parts[index, low : low + row_tile, :] = jnp.dot(
                    x_all[low : low + row_tile, :],
                    w_all[index],
                    preferred_element_type=jnp.float32,
                )
        elif kind == "sum":
            owner = (z + hop) % ring if way == 0 else (z + ring - hop) % ring
            total = parts[index, rows_of(owner), :]
            if runs(way, index, hop + 1, half):
                wait_sum(way, hop + 1, index)
                total = total + sum_in[way, hop, index].astype(jnp.float32)
            sum_out[way, hop - 1, index] = total.astype(jnp.bfloat16)
            send(
                sum_out.at[way, hop - 1, index],
                sum_in.at[way, hop - 1, index],
                sum_sems,
                (way, hop - 1, index),
                step[way],
            )
        elif kind == "act":
            total = parts[index, rows_of(z), :]
            for side_way in range(2):
                wait_sum(side_way, 1, index)
                total = total + sum_in[side_way, 0, index].astype(jnp.float32)
            gate = total[:, :cols]
            act = gate / (1.0 + jnp.exp(-gate)) * total[:, cols:]
            low = (index % per_part) * cols
            hidden[z, index // per_part, :, low : low + cols] = act.astype(jnp.bfloat16)
        elif kind == "gather":
            if hop > 1:
                ready(way, hop - 1, index)
            origin = (z + ring - hop + 1) % ring if way == 0 else (z + hop - 1) % ring
            send(
                hidden.at[origin, index],
                hidden.at[origin, index],
                gather_sems,
                (way, hop - 1, index),
                step[way],
            )
        elif kind == "down":
            if not joined:
                fill_down(d_own, side)
                remote(d_send, d_far, w_sems, (PIECES,), mate).wait_recv()
            if index > 0:
                _, _, source_hop, source_way = sources_of(index, half)[hop]
                ready(source_way, source_hop, hop)
            lhs = hidden[origin_of(index), hop]
            low = hop * part_units
            far = jnp.dot(
                lhs, d_far[low : low + part_units, :], preferred_element_type=jnp.float32
            )
            own = jnp.dot(
                lhs, d_own[low : low + part_units, :], preferred_element_type=jnp.float32
            )
            count = joined[index] = joined.get(index, 0) + 1
            if count > 1:
                far = far + y_far[index]
                own = own + y_own[index]
            y_own[index] = own
            if count < PARTS:
                y_far[index] = far
            else:
                y_out[index] = far.astype(jnp.bfloat16)
                send(y_out.at[index], y_in.at[index], y_sems, (index,), mate)
        else:
            if not told:
                pl.semaphore_wait(spread.at[3], 1)
                told = True
            remote(y_out.at[index], y_in.at[index], y_sems, (index,), mate).wait_recv()
            total = y_own[index] + y_in[index].astype(jnp.float32)
            y_back[index * 8 : index * 8 + 8] = total.reshape(8, 8, width).astype(jnp.bfloat16)
            origin = origin_of(index)
            block = origin // 3
            dst = landed.at[share, expert, origin % 3]
            for other in (4, 3, 5, 2, 6, 1, 7, 0):
                to_y = (y + other) % 8
                src = y_back.at[index * 8 + to_y]
                target = {"expert": (block % 2) * 16 + to_y * 2 + block // 2}
                copy = remote(src, dst, back_sems, (), target)
                if other > 0:
                    copy.start()
                else:
                    pl.when(block != my_block)(copy.start)
                    pl.when(block == my_block)(
                        pltpu.make_async_copy(src, dst, back_sems.at[1]).start
                    )

    wait_bytes(landed, back_sems.at[1])
    sums = landed[0].astype(jnp.float32)
    for index in range(1, 4):
        sums = sums + landed[index].astype(jnp.float32)
    out_ref[...] = lax.dot_general(
        mixing[...],
        sums.reshape(slots, width),
        (((0,), (0,)), ((), ())),
        precision=lax.Precision.HIGHEST,
        preferred_element_type=jnp.float32,
    )

    wait_bytes(packed.at[:7], route_sems.at[0, 0])
    wait_bytes(packed, route_sems.at[0, 1])
    wait_bytes(y_back.at[:93], back_sems.at[0])
    for copy in sends:
        copy.wait_send()


def shards(tokens, expert_ids, gate_values, w_gate, w_up, w_down, scale_gate, scale_up, scale_down):
    ring = lax.axis_size("fsdp") // 2
    local_tokens, width = tokens.shape
    rows = lax.axis_size("expert") * CAP
    units = w_gate.shape[1] // 2
    cols = units // PIECES
    half = ring // 2
    chunk = rows // ring
    vmem = pl.BlockSpec(memory_space=pltpu.VMEM)
    smem = pl.BlockSpec(memory_space=pltpu.SMEM)
    bf16, f32 = jnp.bfloat16, jnp.float32
    dma = pltpu.SemaphoreType.DMA
    anywhere = pl.BlockSpec(memory_space=pl.ANY)
    mixed = pl.pallas_call(
        functools.partial(expert_kernel, ring),
        out_shape=jax.ShapeDtypeStruct((local_tokens, width), f32),
        in_specs=[vmem] * 3 + [anywhere] * 3 + [smem] * 3,
        out_specs=vmem,
        scratch_shapes=[
            pltpu.VMEM(w_gate.shape, bf16),
            pltpu.VMEM(w_up.shape, bf16),
            pltpu.VMEM(w_down.shape, bf16),
            pltpu.VMEM((EXPERTS, 3, 8, width), bf16),
            pltpu.VMEM((EXPERTS * CAP, local_tokens), f32),
            pltpu.VMEM((4, 3, 8, 8, width), bf16),
            pltpu.VMEM((4, 3, 8, 8, width), bf16),
            pltpu.VMEM((rows, 2 * width), bf16),
            pltpu.VMEM((PIECES, width, 2 * cols), bf16),
            pltpu.VMEM((PIECES, 2 * width, 2 * cols), bf16),
            pltpu.VMEM((units, width), bf16),
            pltpu.VMEM((units, width), bf16),
            pltpu.VMEM((units, width), bf16),
            pltpu.VMEM((PIECES, rows, 2 * cols), f32),
            pltpu.VMEM((2, half, PIECES, chunk, 2 * cols), bf16),
            pltpu.VMEM((2, half, PIECES, chunk, 2 * cols), bf16),
            pltpu.VMEM((ring, PARTS, chunk, units // PARTS), bf16),
            pltpu.VMEM((ring, chunk, width), f32),
            pltpu.VMEM((ring, chunk, width), f32),
            pltpu.VMEM((ring, chunk, width), bf16),
            pltpu.VMEM((ring, chunk, width), bf16),
            pltpu.VMEM((ring * 8, 8, width), bf16),
            pltpu.VMEM((4, EXPERTS, 3, 8, width), bf16),
            dma((2, 2)),
            dma((2, 2)),
            dma((2, 2)),
            dma((2, 2)),
            dma((2, PIECES + 1)),
            dma((2, 2, half, PIECES)),
            dma((2, 2, half, PARTS)),
            dma((2, ring)),
            dma((2,)),
            dma((3,)),
            pltpu.SemaphoreType.REGULAR((4,)),
        ],
        compiler_params=pltpu.CompilerParams(collective_id=0, has_side_effects=True),
        name="expert_layer",
    )(
        expert_ids.T,
        gate_values.T,
        tokens,
        w_gate,
        w_up,
        w_down,
        scale_gate,
        scale_up,
        scale_down.T,
    )
    return mixed.astype(bf16)


def solution(mesh):
    in_specs = (
        P("expert", "fsdp"),
        P("expert", None),
        P("expert", None),
        P("fsdp", "expert"),
        P("fsdp", "expert"),
        P("expert", "fsdp"),
        P("fsdp", "expert"),
        P("fsdp", "expert"),
        P("expert", "fsdp"),
    )
    out_specs = P("expert", "fsdp")
    return jax.shard_map(shards, mesh=mesh, in_specs=in_specs, out_specs=out_specs, check_vma=False)
```
